128 devices in a mesh: tm: 4 (over y_hi, core), bank: 16 (over x, z), cuts: 2 (over y_lo).
Axes of the slice: x: 4, y: 4 (y_hi: 2, y_lo: 2; y = y_hi * 2 + y_lo), z: 4, core: 2. Of those that a mesh axis runs over, the one named last changes fastest.
Arguments:
- strain: float32 [2, 8192], P(None, 'tm'), may hold values from -6 to 6
- injections: float32 [8, 2, 512], replicated, may hold values from -12 to 12
- offsets: int32 [8, 2], replicated, may hold values from 0 to 7680
- slot_of: int32 [8192], replicated, may hold values from 0 to 8191, each once
- basis_filters: bfloat16 [16, 8, 256, 128], P('bank', 'cuts'), may hold values from -0.375 to 0.375
- recon_matrix: bfloat16 [16, 8, 128, 1024], P('bank', 'cuts'), may hold values from -0.1875 to 0.1875
Outputs:
- snr: bfloat16 [2, 8192, 2, 8192], P(None, ('tm', 'bank', 'cuts'))
The draws below stay inside these ranges and needn't reach their ends.
All inputs are finite; a program needn't handle non-finite values.
Results may differ from the reference program's by a relative error of at most 0.0057.
Values may be sent and summed in bfloat16 or wider, within the bound.
A program may use at most 128 MiB of HBM per device.

```python
import jax
import jax.numpy as jnp
from jax import lax

DET = 2
TAPS = 256
BASIS = 128
TPL = 512
NINJ = 8
WLEN = 512
NSL = 8
NSUB = 16
TEMPLATES = 8192
TIME = 8192


def set_ends(array, rng, smallest, high):
    dims = array.shape
    spot = [jax.random.randint(jax.random.fold_in(rng, axis), (), 0, dims[axis]) for axis in range(len(dims))]
    array = array.at[tuple(spot)].set(smallest)
    longest = dims.index(max(dims))
    spot[longest] = (spot[longest] + 1) % dims[longest]
    return array.at[tuple(spot)].set(high)


def shard_levels(own_key, extent, split, smallest, top_value):
    factor_of, own = 1.0, jax.random.fold_in(own_key, 6)
    for position, shards_of in split:
        heights = jnp.exp(jax.random.uniform(jax.random.fold_in(own, position), (shards_of,), jnp.float32, smallest / len(split), top_value / len(split)))
        factor_of = factor_of * jnp.repeat(heights, extent[position] // shards_of).reshape([-1 if axis == position else 1 for axis in range(len(extent))])
    return factor_of


def bell_draw(rng, dims, spread, bound, pieces=(), kind=jnp.bfloat16):
    drawn = spread * jax.random.normal(rng, dims, jnp.float32)
    if pieces:
        drawn = drawn * shard_levels(rng, dims, pieces, -0.22, 0.18)
    return jnp.clip(drawn, -bound, bound).astype(kind)


def setup_inputs(seed: int = 0) -> dict:
    key_of = jax.random.split(jax.random.key(seed), 7)
    strain = bell_draw(key_of[0], (DET, TIME), 1.0, 6.0, ((1, 4),), jnp.float32)
    injections = bell_draw(key_of[1], (NINJ, DET, WLEN), 2.0, 12.0, (), jnp.float32)
    offsets = set_ends(jax.random.randint(key_of[2], (NINJ, DET), 0, TIME - WLEN + 1), jax.random.fold_in(key_of[2], 1), 0, TIME - WLEN).astype(jnp.int32)
    slot_of = jax.random.permutation(key_of[3], TEMPLATES).astype(jnp.int32)
    basis_filters = bell_draw(key_of[4], (NSUB, NSL, TAPS, BASIS), TAPS ** -0.5, 0.375, ((0, 16), (1, 2)))
    recon_matrix = bell_draw(key_of[5], (NSUB, NSL, BASIS, 2 * TPL), (BASIS * NSL) ** -0.5, 0.1875, ((0, 16), (1, 2)))
    return dict(strain=strain, injections=injections, offsets=offsets, slot_of=slot_of, basis_filters=basis_filters, recon_matrix=recon_matrix)


def reference(strain, injections, offsets, slot_of, basis_filters, recon_matrix):
    where_at = offsets[:, :, None] + jnp.arange(WLEN, dtype=jnp.int32)[None, None, :]
    detector = jnp.broadcast_to(jnp.arange(DET, dtype=jnp.int32)[None, :, None], where_at.shape)
    injected = strain.at[detector, where_at].add(injections)
    samples = injected.astype(jnp.bfloat16)
    lag_table = jnp.arange(TIME)[:, None] + (TAPS - 1) - jnp.arange(TAPS)[None, :]

    def one_bank(inputs):
        filters, matrices = inputs
        total = jnp.zeros((DET, TIME, 2 * TPL), jnp.float32)
        for index in range(NSL):
            padded = jnp.pad(samples, ((0, 0), (index * TAPS + TAPS - 1, 0)))
            lagged = padded[:, lag_table].astype(jnp.float32)
            basis_out = jnp.einsum("dtk,km->dtm", lagged, filters[index].astype(jnp.float32)).astype(jnp.bfloat16)
            total = total + jnp.einsum("dtm,mc->dtc", basis_out.astype(jnp.float32), matrices[index].astype(jnp.float32))
        return total.astype(jnp.bfloat16)

    slot_snr = lax.map(one_bank, (basis_filters, recon_matrix))
    ordered = slot_snr.reshape(NSUB, DET, TIME, 2, TPL).transpose(1, 2, 3, 0, 4).reshape(DET, TIME, 2, NSUB * TPL)
    return jnp.take(ordered, slot_of, axis=3)
```

```python
import functools

import jax
import jax.numpy as jnp
from jax import lax
from jax.experimental import pallas as pl
from jax.experimental.pallas import tpu as pltpu
from jax.sharding import PartitionSpec as P

MESH = pl.DeviceIdType.MESH
LANES = 128
BLOCK = 64
PIECES = 4
ORDER = (
    (1, 1), (3, 3), (1, 3), (3, 1),
    (1, 0), (3, 0), (0, 1), (0, 3),
    (2, 2), (2, 0), (0, 2),
    (2, 1), (2, 3), (1, 2), (3, 2),
)


def pair_select(dtype):
    row = lax.broadcasted_iota(jnp.int32, (256, 256), 0)
    col = lax.broadcasted_iota(jnp.int32, (256, 256), 1)
    return ((row // 2 == col % LANES) & (row % 2 == col // LANES)).astype(dtype)


def inject_kernel(offsets, strain, injections, out, acc):
    detectors, rows = strain.shape[0], strain.shape[1]
    anchor = lax.axis_index("tm") * (rows * LANES)
    acc[...] = jnp.zeros_like(acc)
    lane = lax.broadcasted_iota(jnp.int32, (8, LANES), 1)
    zeros = jnp.zeros((4, LANES), jnp.float32)
    for d in range(detectors):
        acc[d, pl.ds(8, rows), :] = strain[d]
        for i in range(injections.shape[0]):
            first = offsets[i, d] - anchor
            row = first // LANES
            shift = first - row * LANES
            wave = jnp.concatenate([injections[i, d], zeros], axis=0)
            rolled = pltpu.roll(wave, shift, axis=1)
            placed = jnp.where(lane >= shift, rolled, pltpu.roll(rolled, 1, axis=0))
            where = jnp.clip(row, -8, rows) + 8
            acc[d, pl.ds(where, 8), :] += placed
        out[d] = acc[d, pl.ds(8, rows), :].astype(jnp.bfloat16).astype(jnp.float32)


def inject(strain, injections, offsets):
    detectors, span = strain.shape
    rows = span // LANES
    shaped = strain.reshape(detectors, rows, LANES)
    waves = injections.reshape(*injections.shape[:2], -1, LANES)
    return pl.pallas_call(
        inject_kernel,
        out_shape=jax.ShapeDtypeStruct(shaped.shape, jnp.float32),
        in_specs=[
            pl.BlockSpec(memory_space=pltpu.SMEM),
            pl.BlockSpec(memory_space=pltpu.VMEM),
            pl.BlockSpec(memory_space=pltpu.VMEM),
        ],
        out_specs=pl.BlockSpec(memory_space=pltpu.VMEM),
        scratch_shapes=[pltpu.VMEM((detectors, rows + 16, LANES), jnp.float32)],
    )(offsets, shaped, waves)


def filter_kernel(
    samples, filters, recon, out,
    spans, windows, history, taps, raw, weights, basis, staged,
    local_sem, halo_sem, send_sem, recv_sem, pass_sem, got_sem, out_sem, in_sem,
):
    tm, bank, cuts = lax.axis_index("tm"), lax.axis_index("bank"), lax.axis_index("cuts")
    hi, core = tm // 2, tm % 2
    x, z = bank // 4, bank % 4
    partner = {"tm": hi * 2 + 1 - core}
    beside = ({"cuts": 1 - cuts}, {"tm": (1 - hi) * 2 + core, "cuts": 1 - cuts})
    after, before = {"tm": (tm + 1) % 4}, {"tm": (tm + 3) % 4}

    barrier = pltpu.get_barrier_semaphore()
    for device in (*beside, after, before, *({"bank": (bank + k) % 16} for k in range(1, 16))):
        pl.semaphore_signal(barrier, inc=1, device_id=device, device_id_type=MESH)

    locals_ = [
        pltpu.make_async_copy(filters.at[0], taps.at[pl.ds(4 * cuts, 4)], local_sem.at[0]),
        pltpu.make_async_copy(recon.at[0], raw.at[pl.ds(4 * cuts, 4)], local_sem.at[1]),
        pltpu.make_async_copy(samples, spans.at[1], local_sem.at[2]),
    ]
    for copy in locals_:
        copy.start()
    pl.semaphore_wait(barrier, 19)

    halo = pltpu.make_async_remote_copy(
        samples, spans.at[0], halo_sem.at[0], halo_sem.at[1],
        device_id=after, device_id_type=MESH,
    )
    halo.start()
    sends = []
    for j in range(2):
        mine = 2 * core + j
        for n, (source, target) in enumerate(((filters, taps), (recon, raw))):
            sends.append(pltpu.make_async_remote_copy(
                source.at[0, mine], target.at[4 * cuts + mine],
                send_sem.at[j, n], recv_sem.at[j, n],
                device_id=beside[j], device_id_type=MESH,
            ))
            sends[-1].start()

    locals_[2].wait()
    halo.wait()

    lane = lax.broadcasted_iota(jnp.int32, (32, LANES), 1)
    low = lane < BLOCK
    row32 = lax.broadcasted_iota(jnp.int32, (32, LANES), 0)
    known = (row32 >= 16) | (tm > 0)
    for d in range(2):
        line = jnp.concatenate([spans[0, d], spans[1, d]], axis=0)
        line = jnp.where(known, line, 0.0)
        swapped = pltpu.roll(line, BLOCK, axis=1)
        if d == 1:
            windows[0] = line
            windows[1] = jnp.where(low, swapped, pltpu.roll(swapped, 31, axis=0))
        else:
            windows[2] = swapped
            windows[3] = jnp.where(low, pltpu.roll(line, 31, axis=0), line)
    half = lax.broadcasted_iota(jnp.int32, (BLOCK, LANES), 1) < BLOCK

    def fill(j, carry):
        for odd in range(2):
            row = j if odd else j + cuts
            tile = 60 + cuts - 2 * j if odd else 61 - cuts - 2 * j
            parts = []
            for kind in (2 + odd, odd):
                wide = jnp.broadcast_to(windows[kind, pl.ds(row, 1), :], (BLOCK, LANES))
                parts.append(pltpu.roll(wide, 0, axis=1, stride=1, stride_axis=0))
            value = jnp.where(half, parts[0], parts[1]).astype(jnp.bfloat16)
            history[pl.ds(pl.multiple_of(tile * BLOCK, BLOCK), BLOCK), :] = value
        return carry

    lax.fori_loop(0, 31, fill, 0)

    select = pair_select(jnp.bfloat16)

    def turn(slot):
        for h in range(4):
            pair = jnp.concatenate(
                [raw[slot, :, pl.ds(128 * h, 128)], raw[slot, :, pl.ds(512 + 128 * h, 128)]],
                axis=1,
            )
            turned = lax.dot_general(
                select, pair, (((1,), (1,)), ((), ())), preferred_element_type=jnp.float32
            )
            weights[slot, pl.ds(256 * h, 256), :] = turned.astype(jnp.bfloat16)

    locals_[0].wait()
    locals_[1].wait()
    for i in range(4):
        turn(4 * cuts + i)
    other = 4 * (1 - cuts)
    passes = []
    for n, target in enumerate((taps, raw)):
        for j in range(2):
            sends[2 * j + n].wait_recv()
            held = target.at[other + 2 * core + j]
            passes.append(pltpu.make_async_remote_copy(
                held, held, pass_sem.at[j, n], got_sem.at[j, n],
                device_id=partner, device_id_type=MESH,
            ))
            passes[-1].start()
    for j in range(2):
        turn(other + 2 * core + j)
    for copy in passes:
        copy.wait_recv()
    for j in range(2):
        turn(other + 2 * (1 - core) + j)

    def target_of(k):
        dx, dz = 0, 0
        for i, (a, b) in enumerate(ORDER):
            dx = jnp.where(k == i, a, dx)
            dz = jnp.where(k == i, b, dz)
        return ((x + dx) % 4) * 4 + (z + dz) % 4

    rows = weights.shape[1] // PIECES

    def piece(k, p, h):
        part = pl.ds(h * rows, rows)
        return pltpu.make_async_remote_copy(
            staged.at[k, part], out.at[bank, part], out_sem.at[k, h], in_sem.at[k, h],
            device_id={"bank": p}, device_id_type=MESH,
        )

    def block(k, carry):
        p = target_of(k)
        for s in range(8):
            start = pl.multiple_of(LANES * (15 - p) + 256 * s, LANES)
            made = lax.dot_general(
                taps[s], history[pl.ds(start, 256), :], (((0,), (0,)), ((), ())),
                preferred_element_type=jnp.float32,
            )
            basis[pl.ds(LANES * s, LANES), :] = made.astype(jnp.bfloat16)
        for h in range(PIECES):
            total = jnp.zeros((rows, LANES), jnp.float32)
            for s in range(8):
                total += jnp.dot(
                    weights[s, pl.ds(h * rows, rows), :], basis[pl.ds(LANES * s, LANES), :],
                    preferred_element_type=jnp.float32,
                )
            staged[k, pl.ds(h * rows, rows), :] = total.astype(jnp.bfloat16)

            @pl.when(k < 15)
            def _():
                piece(k, p, h).start()
        return carry

    lax.fori_loop(0, 16, block, 0)
    own = pltpu.make_async_copy(staged.at[15], out.at[bank], local_sem.at[0])
    own.start()

    def finish(k, carry):
        for h in range(PIECES):
            copy = piece(k, target_of(k), h)
            copy.wait_send()
            copy.wait_recv()
        return carry

    lax.fori_loop(0, 15, finish, 0)
    own.wait()
    for copy in (*sends, *passes):
        copy.wait_send()


def filter_and_exchange(samples, filters, recon):
    any_space = pl.BlockSpec(memory_space=pl.ANY)
    columns = recon.shape[3]
    dma = pltpu.SemaphoreType.DMA
    return pl.pallas_call(
        filter_kernel,
        out_shape=jax.ShapeDtypeStruct((16, columns, LANES), jnp.bfloat16),
        in_specs=[any_space] * 3,
        out_specs=any_space,
        scratch_shapes=[
            pltpu.VMEM((2, 2, 16, LANES), jnp.float32),
            pltpu.VMEM((4, 32, LANES), jnp.float32),
            pltpu.VMEM((62 * BLOCK, LANES), jnp.bfloat16),
            pltpu.VMEM((8, 256, 128), jnp.bfloat16),
            pltpu.VMEM((8, 128, columns), jnp.bfloat16),
            pltpu.VMEM((8, columns, 128), jnp.bfloat16),
            pltpu.VMEM((1024, LANES), jnp.bfloat16),
            pltpu.VMEM((16, columns, LANES), jnp.bfloat16),
            dma((3,)), dma((2,)), dma((2, 2)), dma((2, 2)), dma((2, 2)), dma((2, 2)),
            dma((15, PIECES)), dma((15, PIECES)),
        ],
        compiler_params=pltpu.CompilerParams(
            collective_id=0, has_side_effects=True, vmem_limit_bytes=40 * 2**20
        ),
    )(samples, filters, recon)


def order_kernel(width, slots, pairs, out, picked):
    base = pl.program_id(0) * width

    def pick(i, carry):
        for u in range(16):
            picked[i * 16 + u] = pairs[slots[base + i * 16 + u]]
        return carry

    lax.fori_loop(0, width // 16, pick, 0)
    select = pair_select(jnp.bfloat16)
    for j in range(width // 256):
        turned = []
        for h in range(2):
            rows = picked.at[pl.ds(j * 256 + h * 128, 128)].reshape(256, LANES)[...]
            turned.append(lax.dot_general(
                rows, select, (((0,), (0,)), ((), ())), preferred_element_type=jnp.float32
            ).astype(jnp.bfloat16))
        stacked = jnp.concatenate(
            [jnp.concatenate([t[:, q * 128:(q + 1) * 128] for t in turned], axis=1) for q in range(2)],
            axis=0,
        )
        mixed = jnp.dot(select, stacked, preferred_element_type=jnp.float32).astype(jnp.bfloat16)
        out[:, :, :, pl.ds(j * 256, 256)] = mixed.reshape(2, BLOCK, 2, 256)


def put_in_order(slot_of, arrived):
    count = slot_of.shape[0]
    width = 1024
    return pl.pallas_call(
        functools.partial(order_kernel, width),
        out_shape=jax.ShapeDtypeStruct((2, BLOCK, 2, count), jnp.bfloat16),
        grid_spec=pltpu.PrefetchScalarGridSpec(
            num_scalar_prefetch=1,
            grid=(count // width,),
            in_specs=[pl.BlockSpec((count, 2, LANES), lambda i, s: (0, 0, 0))],
            out_specs=pl.BlockSpec((2, BLOCK, 2, width), lambda i, s: (0, 0, 0, i)),
            scratch_shapes=[pltpu.VMEM((width, 2, LANES), jnp.bfloat16)],
        ),
        compiler_params=pltpu.CompilerParams(vmem_limit_bytes=40 * 2**20),
    )(slot_of, arrived.reshape(count, 2, LANES))


def per_device(strain, injections, offsets, slot_of, basis_filters, recon_matrix):
    samples = inject(strain, injections, offsets)
    arrived = filter_and_exchange(samples, basis_filters, recon_matrix)
    return put_in_order(slot_of, arrived)


def solution(mesh):
    return jax.shard_map(
        per_device,
        mesh=mesh,
        in_specs=(
            P(None, "tm"), P(), P(), P(),
            P("bank", "cuts", None, None), P("bank", "cuts", None, None),
        ),
        out_specs=P(None, ("tm", "bank", "cuts"), None, None),
        check_vma=False,
    )
```

```python
import functools

import jax
import jax.numpy as jnp
from jax import lax
from jax.experimental import pallas as pl
from jax.experimental.pallas import tpu as pltpu
from jax.sharding import PartitionSpec as P

MESH = pl.DeviceIdType.MESH
LANES = 128
BLOCK = 64
PIECES = 4
ORDER = (
    (1, 1), (3, 3), (1, 3), (3, 1),
    (1, 0), (3, 0), (0, 1), (0, 3),
    (2, 2), (2, 0), (0, 2),
    (2, 1), (2, 3), (1, 2), (3, 2),
)


def pair_select(dtype):
    row = lax.broadcasted_iota(jnp.int32, (256, 256), 0)
    col = lax.broadcasted_iota(jnp.int32, (256, 256), 1)
    return ((row // 2 == col % LANES) & (row % 2 == col // LANES)).astype(dtype)


def filter_kernel(
    offsets, strain, injections, filters, recon, out,
    spans, waves, windows, history, taps, raw, weights, basis, staged,
    local_sem, halo_sem, send_sem, recv_sem, pass_sem, got_sem, out_sem, in_sem,
):
    tm, bank, cuts = lax.axis_index("tm"), lax.axis_index("bank"), lax.axis_index("cuts")
    hi, core = tm // 2, tm % 2
    x, z = bank // 4, bank % 4
    partner = {"tm": hi * 2 + 1 - core}
    beside = ({"cuts": 1 - cuts}, {"tm": (1 - hi) * 2 + core, "cuts": 1 - cuts})
    after, before = {"tm": (tm + 1) % 4}, {"tm": (tm + 3) % 4}
    other = 4 * (1 - cuts)

    barrier = pltpu.get_barrier_semaphore()
    for device in (*beside, after, before, *({"bank": (bank + k) % 16} for k in range(1, 16))):
        pl.semaphore_signal(barrier, inc=1, device_id=device, device_id_type=MESH)

    locals_ = [
        pltpu.make_async_copy(strain, spans.at[1], local_sem.at[0]),
        pltpu.make_async_copy(injections, waves, local_sem.at[1]),
        pltpu.make_async_copy(recon.at[0], raw.at[pl.ds(4 * cuts, 4)], local_sem.at[2]),
        pltpu.make_async_copy(filters.at[0], taps.at[pl.ds(4 * cuts, 4)], local_sem.at[3]),
    ]
    for copy in locals_:
        copy.start()
    pl.semaphore_wait(barrier, 19)

    def part(n, source, slot):
        if n == 0:
            return (filters.at[0] if source else taps).at[slot]
        h, q = (n - 1) // 2, (n - 1) % 2
        return (recon.at[0] if source else raw).at[slot, :, pl.ds(512 * q + 128 * h, 128)]

    halo = pltpu.make_async_remote_copy(
        strain, spans.at[0], halo_sem.at[0], halo_sem.at[1],
        device_id=after, device_id_type=MESH,
    )
    halo.start()
    sends, passes = {}, {}
    for n in range(1 + 2 * PIECES):
        for j in range(2):
            mine = 2 * core + j
            sends[n, j] = pltpu.make_async_remote_copy(
                part(n, True, mine), part(n, False, 4 * cuts + mine),
                send_sem.at[j, n], recv_sem.at[j, n],
                device_id=beside[j], device_id_type=MESH,
            )
            sends[n, j].start()
            held = part(n, False, other + mine)
            passes[n, j] = pltpu.make_async_remote_copy(
                held, held, pass_sem.at[j, n], got_sem.at[j, n],
                device_id=partner, device_id_type=MESH,
            )

    def pass_on(parts):
        for n in parts:
            for j in range(2):
                sends[n, j].wait_recv()
                passes[n, j].start()

    locals_[0].wait()
    locals_[1].wait()
    halo.wait()

    lane = lax.broadcasted_iota(jnp.int32, (32, LANES), 1)
    row32 = lax.broadcasted_iota(jnp.int32, (32, LANES), 0)
    low = lane < BLOCK
    known = (row32 >= 16) | (tm > 0)
    first_lane = lax.broadcasted_iota(jnp.int32, (1, LANES), 1)
    none = jnp.zeros((1, LANES), jnp.float32)
    for d in range(2):
        line = jnp.concatenate(
            [spans[r // 16, pl.ds(d, 1), pl.ds(LANES * (r % 16), LANES)] for r in range(32)], axis=0
        )
        for i in range(waves.shape[0]):
            first = offsets[d, i] - (tm - 1) * 2048
            row = first // LANES
            shift = first - row * LANES
            turned = [none] + [
                pltpu.roll(waves[i, pl.ds(d, 1), pl.ds(LANES * r, LANES)], shift, axis=1)
                for r in range(4)
            ] + [none]
            for r in range(5):
                placed = jnp.where(first_lane >= shift, turned[r + 1], turned[r])
                line += jnp.where(row32 == row + r, placed, 0.0)
        line = jnp.where(known, line, 0.0).astype(jnp.bfloat16).astype(jnp.float32)
        swapped = pltpu.roll(line, BLOCK, axis=1)
        if d == 1:
            windows[0] = line
            windows[1] = jnp.where(low, swapped, pltpu.roll(swapped, 31, axis=0))
        else:
            windows[2] = swapped
            windows[3] = jnp.where(low, pltpu.roll(line, 31, axis=0), line)
    half = lax.broadcasted_iota(jnp.int32, (BLOCK, LANES), 1) < BLOCK

    def fill(j, carry):
        for odd in range(2):
            row = j if odd else j + cuts
            tile = 60 + cuts - 2 * j if odd else 61 - cuts - 2 * j
            sides = []
            for kind in (2 + odd, odd):
                wide = jnp.broadcast_to(windows[kind, pl.ds(row, 1), :], (BLOCK, LANES))
                sides.append(pltpu.roll(wide, 0, axis=1, stride=1, stride_axis=0))
            value = jnp.where(half, sides[0], sides[1]).astype(jnp.bfloat16)
            history[pl.ds(pl.multiple_of(tile * BLOCK, BLOCK), BLOCK), :] = value
        return carry

    lax.fori_loop(0, 31, fill, 0)

    select = pair_select(jnp.bfloat16)

    def turn(h, slot):
        pair = jnp.concatenate(
            [raw[slot, :, pl.ds(128 * h, 128)], raw[slot, :, pl.ds(512 + 128 * h, 128)]], axis=1
        )
        turned = lax.dot_general(
            select, pair, (((1,), (1,)), ((), ())), preferred_element_type=jnp.float32
        )
        where = pl.ds(pl.multiple_of(LANES * slot, LANES), LANES)
        weights[h, :, where] = turned.astype(jnp.bfloat16)

    pass_on((0, 1, 2))
    locals_[2].wait()
    locals_[3].wait()
    for h in range(PIECES):
        for i in range(4):
            turn(h, 4 * cuts + i)

    def target_of(k):
        dx, dz = 0, 0
        for i, (a, b) in enumerate(ORDER):
            dx = jnp.where(k == i, a, dx)
            dz = jnp.where(k == i, b, dz)
        return ((x + dx) % 4) * 4 + (z + dz) % 4

    rows = weights.shape[1]

    def piece(k, h):
        lines = pl.ds(h * rows, rows)
        return pltpu.make_async_remote_copy(
            staged.at[k, lines], out.at[bank, lines], out_sem.at[k, h], in_sem.at[k, h],
            device_id={"bank": target_of(k)}, device_id_type=MESH,
        )

    def two_blocks(h, i, carry):
        if h == 0:
            places = [LANES * (15 - target_of(2 * i + b)) for b in range(2)]
            for s in range(8):
                past = jnp.concatenate(
                    [history[pl.ds(pl.multiple_of(p + 256 * s, LANES), 256), :] for p in places],
                    axis=1,
                )
                made = lax.dot_general(
                    taps[s], past, (((0,), (0,)), ((), ())), preferred_element_type=jnp.float32
                )
                basis[i, pl.ds(LANES * s, LANES), :] = made.astype(jnp.bfloat16)
        made = jnp.dot(weights[h], basis[i], preferred_element_type=jnp.float32)
        made = made.astype(jnp.bfloat16)
        for b in range(2):
            staged[2 * i + b, pl.ds(h * rows, rows), :] = made[:, LANES * b:LANES * (b + 1)]
        piece(2 * i, h).start()

        @pl.when(i < 7)
        def _():
            piece(2 * i + 1, h).start()

        if h + 1 < PIECES:
            @pl.when(i == 3)
            def _():
                pass_on((3 + 2 * h, 4 + 2 * h))
        return carry

    for h in range(PIECES):
        for n in ((0, 1, 2) if h == 0 else (1 + 2 * h, 2 + 2 * h)):
            for j in range(2):
                passes[n, j].wait_recv()
        for i in range(4):
            turn(h, other + i)
        lax.fori_loop(0, 8, functools.partial(two_blocks, h), 0)
    own = pltpu.make_async_copy(staged.at[15], out.at[bank], local_sem.at[0])
    own.start()

    def finish(k, carry):
        for h in range(PIECES):
            copy = piece(k, h)
            copy.wait_send()
            copy.wait_recv()
        return carry

    lax.fori_loop(0, 15, finish, 0)
    own.wait()
    for copy in (*sends.values(), *passes.values()):
        copy.wait_send()


def filter_and_exchange(strain, injections, offsets, filters, recon):
    hbm = pl.BlockSpec(memory_space=pltpu.HBM)
    columns = recon.shape[3]
    dma = pltpu.SemaphoreType.DMA
    parts = (2, 1 + 2 * PIECES)
    return pl.pallas_call(
        filter_kernel,
        out_shape=jax.ShapeDtypeStruct((16, columns, LANES), jnp.bfloat16),
        in_specs=[pl.BlockSpec(memory_space=pltpu.SMEM)] + [hbm] * 4,
        out_specs=pl.BlockSpec(memory_space=pl.ANY),
        scratch_shapes=[
            pltpu.VMEM((2, *strain.shape), jnp.float32),
            pltpu.VMEM(injections.shape, jnp.float32),
            pltpu.VMEM((4, 32, LANES), jnp.float32),
            pltpu.VMEM((62 * BLOCK, LANES), jnp.bfloat16),
            pltpu.VMEM((8, 256, 128), jnp.bfloat16),
            pltpu.VMEM((8, 128, columns), jnp.bfloat16),
            pltpu.VMEM((PIECES, columns // PIECES, 1024), jnp.bfloat16),
            pltpu.VMEM((8, 1024, 2 * LANES), jnp.bfloat16),
            pltpu.VMEM((16, columns, LANES), jnp.bfloat16),
            dma((4,)), dma((2,)), dma(parts), dma(parts), dma(parts), dma(parts),
            dma((15, PIECES)), dma((15, PIECES)),
        ],
        compiler_params=pltpu.CompilerParams(
            collective_id=0, has_side_effects=True, vmem_limit_bytes=40 * 2**20
        ),
    )(offsets.T, *(pltpu.with_memory_space_constraint(a, pltpu.HBM) for a in (strain, injections, filters, recon)))


def order_kernel(width, slots, pairs, out, picked):
    base = pl.program_id(0) * width

    def pick(i, carry):
        for u in range(16):
            picked[i * 16 + u] = pairs[slots[base + i * 16 + u]]
        return carry

    lax.fori_loop(0, width // 16, pick, 0)
    select = pair_select(jnp.bfloat16)
    for j in range(width // 256):
        turned = []
        for h in range(2):
            rows = picked.at[pl.ds(j * 256 + h * 128, 128)].reshape(256, LANES)[...]
            turned.append(lax.dot_general(
                rows, select, (((0,), (0,)), ((), ())), preferred_element_type=jnp.float32
            ).astype(jnp.bfloat16))
        stacked = jnp.concatenate(
            [jnp.concatenate([t[:, q * 128:(q + 1) * 128] for t in turned], axis=1) for q in range(2)],
            axis=0,
        )
        mixed = jnp.dot(select, stacked, preferred_element_type=jnp.float32).astype(jnp.bfloat16)
        out[:, :, :, pl.ds(j * 256, 256)] = mixed.reshape(2, BLOCK, 2, 256)


def put_in_order(slot_of, arrived):
    count = slot_of.shape[0]
    width = 1024
    return pl.pallas_call(
        functools.partial(order_kernel, width),
        out_shape=jax.ShapeDtypeStruct((2, BLOCK, 2, count), jnp.bfloat16),
        grid_spec=pltpu.PrefetchScalarGridSpec(
            num_scalar_prefetch=1,
            grid=(count // width,),
            in_specs=[pl.BlockSpec((count, 2, LANES), lambda i, s: (0, 0, 0))],
            out_specs=pl.BlockSpec((2, BLOCK, 2, width), lambda i, s: (0, 0, 0, i)),
            scratch_shapes=[pltpu.VMEM((width, 2, LANES), jnp.bfloat16)],
        ),
        compiler_params=pltpu.CompilerParams(vmem_limit_bytes=40 * 2**20),
    )(slot_of, arrived.reshape(count, 2, LANES))


def per_device(strain, injections, offsets, slot_of, basis_filters, recon_matrix):
    arrived = filter_and_exchange(strain, injections, offsets, basis_filters, recon_matrix)
    return put_in_order(slot_of, arrived)


def solution(mesh):
    return jax.shard_map(
        per_device,
        mesh=mesh,
        in_specs=(
            P(None, "tm"), P(), P(), P(),
            P("bank", "cuts", None, None), P("bank", "cuts", None, None),
        ),
        out_specs=P(None, ("tm", "bank", "cuts"), None, None),
        check_vma=False,
    )
```

```python
import functools

import jax
import jax.numpy as jnp
from jax import lax
from jax.experimental import pallas as pl
from jax.experimental.pallas import tpu as pltpu
from jax.sharding import PartitionSpec as P

MESH = pl.DeviceIdType.MESH
LANES = 128
BLOCK = 64
PIECES = 4
ORDER = (
    (2, 1), (2, 3), (1, 2), (3, 2),
    (2, 2), (2, 0), (0, 2),
    (1, 1), (3, 3), (1, 3), (3, 1),
    (1, 0), (3, 0), (0, 1), (0, 3),
)


def pair_select(dtype):
    row = lax.broadcasted_iota(jnp.int32, (256, 256), 0)
    col = lax.broadcasted_iota(jnp.int32, (256, 256), 1)
    return ((row // 2 == col % LANES) & (row % 2 == col // LANES)).astype(dtype)


def filter_kernel(
    offsets, strain, injections, filters, recon, out,
    spans, waves, windows, history, taps, raw, weights, basis, staged,
    local_sem, halo_sem, send_sem, recv_sem, pass_sem, got_sem, out_sem, in_sem,
):
    tm, bank, cuts = lax.axis_index("tm"), lax.axis_index("bank"), lax.axis_index("cuts")
    hi, core = tm // 2, tm % 2
    x, z = bank // 4, bank % 4
    partner = {"tm": hi * 2 + 1 - core}
    beside = ({"cuts": 1 - cuts}, {"tm": (1 - hi) * 2 + core, "cuts": 1 - cuts})
    after, before = {"tm": (tm + 1) % 4}, {"tm": (tm + 3) % 4}
    other = 4 * (1 - cuts)

    barrier = pltpu.get_barrier_semaphore()
    for device in (*beside, after, before, *({"bank": (bank + k) % 16} for k in range(1, 16))):
        pl.semaphore_signal(barrier, inc=1, device_id=device, device_id_type=MESH)

    locals_ = [
        pltpu.make_async_copy(strain, spans.at[1], local_sem.at[0]),
        pltpu.make_async_copy(injections, waves, local_sem.at[1]),
        pltpu.make_async_copy(recon.at[0], raw.at[pl.ds(4 * cuts, 4)], local_sem.at[2]),
        pltpu.make_async_copy(filters.at[0], taps.at[pl.ds(4 * cuts, 4)], local_sem.at[3]),
    ]
    for copy in locals_:
        copy.start()
    pl.semaphore_wait(barrier, 19)

    def part(n, source, slot):
        if n == 0:
            return (filters.at[0] if source else taps).at[slot]
        h, q = (n - 1) // 2, (n - 1) % 2
        return (recon.at[0] if source else raw).at[slot, :, pl.ds(512 * q + 128 * h, 128)]

    halo = pltpu.make_async_remote_copy(
        strain, spans.at[0], halo_sem.at[0], halo_sem.at[1],
        device_id=after, device_id_type=MESH,
    )
    halo.start()
    sends, passes = {}, {}
    for n in range(1 + 2 * PIECES):
        for j in range(2):
            mine = 2 * core + j
            sends[n, j] = pltpu.make_async_remote_copy(
                part(n, True, mine), part(n, False, 4 * cuts + mine),
                send_sem.at[j, n], recv_sem.at[j, n],
                device_id=beside[j], device_id_type=MESH,
            )
            sends[n, j].start()
            held = part(n, False, other + mine)
            passes[n, j] = pltpu.make_async_remote_copy(
                held, held, pass_sem.at[j, n], got_sem.at[j, n],
                device_id=partner, device_id_type=MESH,
            )

    def pass_on(parts):
        for n in parts:
            for j in range(2):
                sends[n, j].wait_recv()
                passes[n, j].start()

    locals_[0].wait()
    locals_[1].wait()
    halo.wait()

    lane = lax.broadcasted_iota(jnp.int32, (32, LANES), 1)
    row32 = lax.broadcasted_iota(jnp.int32, (32, LANES), 0)
    low = lane < BLOCK
    known = (row32 >= 16) | (tm > 0)
    first_lane = lax.broadcasted_iota(jnp.int32, (1, LANES), 1)
    none = jnp.zeros((1, LANES), jnp.float32)
    for d in range(2):
        line = jnp.concatenate(
            [spans[r // 16, pl.ds(d, 1), pl.ds(LANES * (r % 16), LANES)] for r in range(32)], axis=0
        )
        for i in range(waves.shape[0]):
            first = offsets[d, i] - (tm - 1) * 2048
            row = first // LANES
            shift = first - row * LANES
            turned = [none] + [
                pltpu.roll(waves[i, pl.ds(d, 1), pl.ds(LANES * r, LANES)], shift, axis=1)
                for r in range(4)
            ] + [none]
            for r in range(5):
                placed = jnp.where(first_lane >= shift, turned[r + 1], turned[r])
                line += jnp.where(row32 == row + r, placed, 0.0)
        line = jnp.where(known, line, 0.0).astype(jnp.bfloat16).astype(jnp.float32)
        swapped = pltpu.roll(line, BLOCK, axis=1)
        if d == 1:
            windows[0] = line
            windows[1] = jnp.where(low, swapped, pltpu.roll(swapped, 31, axis=0))
        else:
            windows[2] = swapped
            windows[3] = jnp.where(low, pltpu.roll(line, 31, axis=0), line)
    half = lax.broadcasted_iota(jnp.int32, (BLOCK, LANES), 1) < BLOCK

    def fill(j, carry):
        for odd in range(2):
            row = j if odd else j + cuts
            tile = 60 + cuts - 2 * j if odd else 61 - cuts - 2 * j
            sides = []
            for kind in (2 + odd, odd):
                wide = jnp.broadcast_to(windows[kind, pl.ds(row, 1), :], (BLOCK, LANES))
                sides.append(pltpu.roll(wide, 0, axis=1, stride=1, stride_axis=0))
            value = jnp.where(half, sides[0], sides[1]).astype(jnp.bfloat16)
            history[pl.ds(pl.multiple_of(tile * BLOCK, BLOCK), BLOCK), :] = value
        return carry

    lax.fori_loop(0, 31, fill, 0)

    select = pair_select(jnp.bfloat16)

    def turn(h, slot):
        pair = jnp.concatenate(
            [raw[slot, :, pl.ds(128 * h, 128)], raw[slot, :, pl.ds(512 + 128 * h, 128)]], axis=1
        )
        turned = lax.dot_general(
            select, pair, (((1,), (1,)), ((), ())), preferred_element_type=jnp.float32
        )
        where = pl.ds(pl.multiple_of(LANES * slot, LANES), LANES)
        weights[h, :, where] = turned.astype(jnp.bfloat16)

    pass_on((0, 1, 2))
    locals_[2].wait()
    locals_[3].wait()
    for h in range(PIECES):
        for i in range(4):
            turn(h, 4 * cuts + i)

    def target_of(k):
        dx, dz = 0, 0
        for i, (a, b) in enumerate(ORDER):
            dx = jnp.where(k == i, a, dx)
            dz = jnp.where(k == i, b, dz)
        return ((x + dx) % 4) * 4 + (z + dz) % 4

    rows = weights.shape[1]

    def piece(k, h):
        lines = pl.ds(h * rows, rows)
        return pltpu.make_async_remote_copy(
            staged.at[k, lines], out.at[bank, lines], out_sem.at[k, h], in_sem.at[k, h],
            device_id={"bank": target_of(k)}, device_id_type=MESH,
        )

    def two_blocks(h, i, carry):
        if h == 0:
            places = [LANES * (15 - target_of(2 * i + b)) for b in range(2)]
            for s in range(8):
                past = jnp.concatenate(
                    [history[pl.ds(pl.multiple_of(p + 256 * s, LANES), 256), :] for p in places],
                    axis=1,
                )
                made = lax.dot_general(
                    taps[s], past, (((0,), (0,)), ((), ())), preferred_element_type=jnp.float32
                )
                basis[i, pl.ds(LANES * s, LANES), :] = made.astype(jnp.bfloat16)
        made = jnp.dot(weights[h], basis[i], preferred_element_type=jnp.float32)
        made = made.astype(jnp.bfloat16)
        for b in range(2):
            staged[2 * i + b, pl.ds(h * rows, rows), :] = made[:, LANES * b:LANES * (b + 1)]
        piece(2 * i, h).start()

        @pl.when(i < 7)
        def _():
            piece(2 * i + 1, h).start()

        if h + 1 < PIECES:
            @pl.when(i == 3)
            def _():
                pass_on((3 + 2 * h, 4 + 2 * h))
        return carry

    for h in range(PIECES):
        for n in ((0, 1, 2) if h == 0 else (1 + 2 * h, 2 + 2 * h)):
            for j in range(2):
                passes[n, j].wait_recv()
        for i in range(4):
            turn(h, other + i)
        lax.fori_loop(0, 8, functools.partial(two_blocks, h), 0)
    own = pltpu.make_async_copy(staged.at[15], out.at[bank], local_sem.at[0])
    own.start()

    def finish(k, carry):
        for h in range(PIECES):
            copy = piece(k, h)
            copy.wait_send()
            copy.wait_recv()
        return carry

    lax.fori_loop(0, 15, finish, 0)
    own.wait()
    for copy in (*sends.values(), *passes.values()):
        copy.wait_send()


def filter_and_exchange(strain, injections, offsets, filters, recon):
    hbm = pl.BlockSpec(memory_space=pltpu.HBM)
    columns = recon.shape[3]
    dma = pltpu.SemaphoreType.DMA
    parts = (2, 1 + 2 * PIECES)
    return pl.pallas_call(
        filter_kernel,
        out_shape=jax.ShapeDtypeStruct((16, columns, LANES), jnp.bfloat16),
        in_specs=[pl.BlockSpec(memory_space=pltpu.SMEM)] + [hbm] * 4,
        out_specs=pl.BlockSpec(memory_space=pl.ANY),
        scratch_shapes=[
            pltpu.VMEM((2, *strain.shape), jnp.float32),
            pltpu.VMEM(injections.shape, jnp.float32),
            pltpu.VMEM((4, 32, LANES), jnp.float32),
            pltpu.VMEM((62 * BLOCK, LANES), jnp.bfloat16),
            pltpu.VMEM((8, 256, 128), jnp.bfloat16),
            pltpu.VMEM((8, 128, columns), jnp.bfloat16),
            pltpu.VMEM((PIECES, columns // PIECES, 1024), jnp.bfloat16),
            pltpu.VMEM((8, 1024, 2 * LANES), jnp.bfloat16),
            pltpu.VMEM((16, columns, LANES), jnp.bfloat16),
            dma((4,)), dma((2,)), dma(parts), dma(parts), dma(parts), dma(parts),
            dma((15, PIECES)), dma((15, PIECES)),
        ],
        compiler_params=pltpu.CompilerParams(
            collective_id=0, has_side_effects=True, vmem_limit_bytes=40 * 2**20
        ),
    )(offsets.T, *(pltpu.with_memory_space_constraint(a, pltpu.HBM) for a in (strain, injections, filters, recon)))


def pick_kernel(slots, pairs, out, even, odd, sem):
    width = even.shape[0]
    count = slots.shape[0] // width
    held = (even, odd)

    def fetch(c, b):
        lines = pl.ds(pl.multiple_of(c * width, width), width)
        return pltpu.make_async_copy(slots.at[lines], held[b], sem.at[b])

    for b in range(2):
        fetch(b, b).start()

    def step(i, carry):
        for b in range(2):
            c = 2 * i + b
            fetch(c, b).wait()
            base = c * width
            for u in range(width):
                out[base + u] = pairs[held[b][u]]

            @pl.when(c + 2 < count)
            def _():
                fetch(c + 2, b).start()
        return carry

    lax.fori_loop(0, count // 2, step, 0)


def turn_kernel(picked, out, select, spread):
    @pl.when(pl.program_id(0) == 0)
    def _():
        select[...] = pair_select(jnp.bfloat16)
        row = lax.broadcasted_iota(jnp.int32, (256, 256), 0)
        col = lax.broadcasted_iota(jnp.int32, (256, 256), 1)
        spread[...] = ((row // 16 == col % 16) & (row % 16 == col // 16)).astype(jnp.bfloat16)

    for g in range(picked.shape[0] // 2048):
        tiles = []
        for j in range(8):
            tiles.append(lax.dot_general(
                picked[pl.ds((8 * g + j) * 256, 256), :], select[...], (((0,), (0,)), ((), ())),
                preferred_element_type=jnp.float32,
            ).astype(jnp.bfloat16))
        for t in range(0, 8, 2):
            sides = [
                jnp.concatenate(
                    [tiles[j][16 * u:16 * u + 16, 128 * q:128 * q + 128]
                     for j in range(8) for q in range(2)],
                    axis=0,
                )
                for u in (t, t + 1)
            ]
            mixed = jnp.dot(
                spread[...], jnp.concatenate(sides, axis=1), preferred_element_type=jnp.float32
            ).astype(jnp.bfloat16)
            for h in range(2):
                out[pl.ds(16 * (t + h), 16), pl.ds(16 * g, 16), :] = (
                    mixed[:, 128 * h:128 * h + 128].reshape(16, 16, LANES)
                )


def put_in_order(slot_of, arrived):
    count = slot_of.shape[0]
    width, step = 1024, 2048
    vmem = pl.BlockSpec(memory_space=pltpu.VMEM)
    picked = pl.pallas_call(
        pick_kernel,
        out_shape=jax.ShapeDtypeStruct((count, 2, LANES), jnp.bfloat16),
        in_specs=[pl.BlockSpec(memory_space=pl.ANY), vmem],
        out_specs=vmem,
        scratch_shapes=[pltpu.SMEM((width,), jnp.int32)] * 2 + [pltpu.SemaphoreType.DMA((2,))],
        compiler_params=pltpu.CompilerParams(vmem_limit_bytes=40 * 2**20),
    )(slot_of, arrived.reshape(count, 2, LANES))
    tiles = count // LANES
    turned = pl.pallas_call(
        turn_kernel,
        out_shape=jax.ShapeDtypeStruct((2 * BLOCK, 2 * tiles, LANES), jnp.bfloat16),
        grid=(count // step,),
        in_specs=[pl.BlockSpec((2 * step, LANES), lambda i: (i, 0))],
        out_specs=pl.BlockSpec((2 * BLOCK, step // BLOCK, LANES), lambda i: (0, i, 0)),
        scratch_shapes=[pltpu.VMEM((256, 256), jnp.bfloat16)] * 2,
        compiler_params=pltpu.CompilerParams(vmem_limit_bytes=40 * 2**20),
    )(picked.reshape(2 * count, LANES))
    turned = turned.reshape(2 * BLOCK, tiles, 2, LANES).transpose(0, 2, 1, 3)
    return turned.reshape(2, BLOCK, 2, count)


def per_device(strain, injections, offsets, slot_of, basis_filters, recon_matrix):
    arrived = filter_and_exchange(strain, injections, offsets, basis_filters, recon_matrix)
    return put_in_order(slot_of, arrived)


def solution(mesh):
    return jax.shard_map(
        per_device,
        mesh=mesh,
        in_specs=(
            P(None, "tm"), P(), P(), P(),
            P("bank", "cuts", None, None), P("bank", "cuts", None, None),
        ),
        out_specs=P(None, ("tm", "bank", "cuts"), None, None),
        check_vma=False,
    )
```

```python
import functools

import jax
import jax.numpy as jnp
from jax import lax
from jax.experimental import pallas as pl
from jax.experimental.pallas import tpu as pltpu
from jax.sharding import PartitionSpec as P

MESH = pl.DeviceIdType.MESH
LANES = 128
BLOCK = 64
PIECES = 4
EARLY = 1
ORDER = (
    (2, 1), (2, 3), (1, 2), (3, 2),
    (2, 2), (2, 0), (0, 2),
    (1, 1), (3, 3), (1, 3), (3, 1),
    (1, 0), (3, 0), (0, 1), (0, 3),
)


def pair_select(dtype):
    row = lax.broadcasted_iota(jnp.int32, (256, 256), 0)
    col = lax.broadcasted_iota(jnp.int32, (256, 256), 1)
    return ((row // 2 == col % LANES) & (row % 2 == col // LANES)).astype(dtype)


def filter_kernel(
    offsets, strain, injections, filters, recon, out,
    places, spans, waves, windows, history, taps, raw, weights, basis, staged,
    local_sem, halo_sem, send_sem, recv_sem, pass_sem, got_sem, out_sem, in_sem,
):
    tm, bank, cuts = lax.axis_index("tm"), lax.axis_index("bank"), lax.axis_index("cuts")
    hi, core = tm // 2, tm % 2
    x, z = bank // 4, bank % 4
    partner = {"tm": hi * 2 + 1 - core}
    beside = ({"cuts": 1 - cuts}, {"tm": (1 - hi) * 2 + core, "cuts": 1 - cuts})
    after, before = {"tm": (tm + 1) % 4}, {"tm": (tm + 3) % 4}
    other = 4 * (1 - cuts)

    barrier = pltpu.get_barrier_semaphore()
    for device in (*beside, after, before, *({"bank": (bank + k) % 16} for k in range(1, 16))):
        pl.semaphore_signal(barrier, inc=1, device_id=device, device_id_type=MESH)

    locals_ = [
        pltpu.make_async_copy(strain, spans.at[1], local_sem.at[0]),
        pltpu.make_async_copy(injections, waves, local_sem.at[1]),
        pltpu.make_async_copy(recon.at[0], raw.at[pl.ds(4 * cuts, 4)], local_sem.at[2]),
        pltpu.make_async_copy(filters.at[0], taps.at[pl.ds(4 * cuts, 4)], local_sem.at[3]),
        pltpu.make_async_copy(offsets, places, local_sem.at[4]),
    ]
    for copy in locals_:
        copy.start()
    pl.semaphore_wait(barrier, 19)

    def part(n, source, slot):
        if n == 0:
            return (filters.at[0] if source else taps).at[slot]
        h, q = (n - 1) // 2, (n - 1) % 2
        return (recon.at[0] if source else raw).at[slot, :, pl.ds(512 * q + 128 * h, 128)]

    halo = pltpu.make_async_remote_copy(
        strain, spans.at[0], halo_sem.at[0], halo_sem.at[1],
        device_id=after, device_id_type=MESH,
    )
    halo.start()
    sends, passes = {}, {}
    for n in range(1 + 2 * PIECES):
        for j in range(2):
            mine = 2 * core + j
            sends[n, j] = pltpu.make_async_remote_copy(
                part(n, True, mine), part(n, False, 4 * cuts + mine),
                send_sem.at[j, n], recv_sem.at[j, n],
                device_id=beside[j], device_id_type=MESH,
            )
            sends[n, j].start()
            held = part(n, False, other + mine)
            passes[n, j] = pltpu.make_async_remote_copy(
                held, held, pass_sem.at[j, n], got_sem.at[j, n],
                device_id=partner, device_id_type=MESH,
            )

    def pass_on(parts):
        for n in parts:
            for j in range(2):
                sends[n, j].wait_recv()
                passes[n, j].start()

    locals_[0].wait()
    locals_[1].wait()
    locals_[4].wait()
    halo.wait()

    lane = lax.broadcasted_iota(jnp.int32, (32, LANES), 1)
    row32 = lax.broadcasted_iota(jnp.int32, (32, LANES), 0)
    low = lane < BLOCK
    known = (row32 >= 16) | (tm > 0)
    first_lane = lax.broadcasted_iota(jnp.int32, (1, LANES), 1)
    none = jnp.zeros((1, LANES), jnp.float32)
    for d in range(2):
        line = jnp.concatenate(
            [spans[r // 16, pl.ds(d, 1), pl.ds(LANES * (r % 16), LANES)] for r in range(32)], axis=0
        )
        for i in range(waves.shape[0]):
            first = places[d, i] - (tm - 1) * 2048
            row = first // LANES
            shift = first - row * LANES
            turned = [none] + [
                pltpu.roll(waves[i, pl.ds(d, 1), pl.ds(LANES * r, LANES)], shift, axis=1)
                for r in range(4)
            ] + [none]
            for r in range(5):
                placed = jnp.where(first_lane >= shift, turned[r + 1], turned[r])
                line += jnp.where(row32 == row + r, placed, 0.0)
        line = jnp.where(known, line, 0.0).astype(jnp.bfloat16).astype(jnp.float32)
        swapped = pltpu.roll(line, BLOCK, axis=1)
        if d == 1:
            windows[0] = line
            windows[1] = jnp.where(low, swapped, pltpu.roll(swapped, 31, axis=0))
        else:
            windows[2] = swapped
            windows[3] = jnp.where(low, pltpu.roll(line, 31, axis=0), line)
    half = lax.broadcasted_iota(jnp.int32, (BLOCK, LANES), 1) < BLOCK

    def fill(j, carry):
        for odd in range(2):
            row = j if odd else j + cuts
            tile = 60 + cuts - 2 * j if odd else 61 - cuts - 2 * j
            sides = []
            for kind in (2 + odd, odd):
                wide = jnp.broadcast_to(windows[kind, pl.ds(row, 1), :], (BLOCK, LANES))
                sides.append(pltpu.roll(wide, 0, axis=1, stride=1, stride_axis=0))
            value = jnp.where(half, sides[0], sides[1]).astype(jnp.bfloat16)
            history[pl.ds(pl.multiple_of(tile * BLOCK, BLOCK), BLOCK), :] = value
        return carry

    lax.fori_loop(0, 31, fill, 0)

    select = pair_select(jnp.bfloat16)

    def turn(h, slot):
        pair = jnp.concatenate(
            [raw[slot, :, pl.ds(128 * h, 128)], raw[slot, :, pl.ds(512 + 128 * h, 128)]], axis=1
        )
        turned = lax.dot_general(
            select, pair, (((1,), (1,)), ((), ())), preferred_element_type=jnp.float32
        )
        where = pl.ds(pl.multiple_of(LANES * slot, LANES), LANES)
        weights[h, :, where] = turned.astype(jnp.bfloat16)

    def target_of(k):
        dx, dz = 0, 0
        for i, (a, b) in enumerate(ORDER):
            dx = jnp.where(k == i, a, dx)
            dz = jnp.where(k == i, b, dz)
        return ((x + dx) % 4) * 4 + (z + dz) % 4

    rows = weights.shape[1]

    def piece(k, h):
        lines = pl.ds(h * rows, rows)
        return pltpu.make_async_remote_copy(
            staged.at[k, lines], out.at[bank, lines], out_sem.at[k, h], in_sem.at[k, h],
            device_id={"bank": target_of(k)}, device_id_type=MESH,
        )

    def make_basis(i):
        starts = [LANES * (15 - target_of(2 * i + b)) for b in range(2)]
        for s in range(8):
            past = jnp.concatenate(
                [history[pl.ds(pl.multiple_of(p + 256 * s, LANES), 256), :] for p in starts],
                axis=1,
            )
            made = lax.dot_general(
                taps[s], past, (((0,), (0,)), ((), ())), preferred_element_type=jnp.float32
            )
            basis[i, pl.ds(LANES * s, LANES), :] = made.astype(jnp.bfloat16)

    def early(i, carry):
        make_basis(i)
        return carry

    def two_blocks(h, i, carry):
        if h == 0:
            @pl.when(i >= EARLY)
            def _():
                make_basis(i)
        made = jnp.dot(weights[h], basis[i], preferred_element_type=jnp.float32)
        made = made.astype(jnp.bfloat16)
        for b in range(2):
            staged[2 * i + b, pl.ds(h * rows, rows), :] = made[:, LANES * b:LANES * (b + 1)]
        piece(2 * i, h).start()

        @pl.when(i < 7)
        def _():
            piece(2 * i + 1, h).start()

        if h + 1 < PIECES:
            @pl.when(i == 3)
            def _():
                pass_on((3 + 2 * h, 4 + 2 * h))
        return carry

    pass_on((0,))
    locals_[2].wait()
    locals_[3].wait()
    for i in range(4):
        turn(0, 4 * cuts + i)
    for j in range(2):
        passes[0, j].wait_recv()
    lax.fori_loop(0, EARLY, early, 0)
    pass_on((1, 2))
    for i in range(2):
        turn(0, other + 2 * core + i)
    for h in range(PIECES):
        for n in (1 + 2 * h, 2 + 2 * h):
            for j in range(2):
                passes[n, j].wait_recv()
        if h == 0:
            for i in range(2):
                turn(0, other + 2 * (1 - core) + i)
        else:
            for i in range(8):
                turn(h, i)
        lax.fori_loop(0, 8, functools.partial(two_blocks, h), 0)
    own = pltpu.make_async_copy(staged.at[15], out.at[bank], local_sem.at[0])
    own.start()

    def finish(k, carry):
        for h in range(PIECES):
            copy = piece(k, h)
            copy.wait_send()
            copy.wait_recv()
        return carry

    lax.fori_loop(0, 15, finish, 0)
    own.wait()
    for copy in (*sends.values(), *passes.values()):
        copy.wait_send()


def filter_and_exchange(strain, injections, offsets, filters, recon):
    hbm = pl.BlockSpec(memory_space=pltpu.HBM)
    columns = recon.shape[3]
    dma = pltpu.SemaphoreType.DMA
    parts = (2, 1 + 2 * PIECES)
    return pl.pallas_call(
        filter_kernel,
        out_shape=jax.ShapeDtypeStruct((16, columns, LANES), jnp.bfloat16),
        in_specs=[hbm] * 5,
        out_specs=pl.BlockSpec(memory_space=pl.ANY),
        scratch_shapes=[
            pltpu.SMEM(offsets.shape[::-1], jnp.int32),
            pltpu.VMEM((2, *strain.shape), jnp.float32),
            pltpu.VMEM(injections.shape, jnp.float32),
            pltpu.VMEM((4, 32, LANES), jnp.float32),
            pltpu.VMEM((62 * BLOCK, LANES), jnp.bfloat16),
            pltpu.VMEM((8, 256, 128), jnp.bfloat16),
            pltpu.VMEM((8, 128, columns), jnp.bfloat16),
            pltpu.VMEM((PIECES, columns // PIECES, 1024), jnp.bfloat16),
            pltpu.VMEM((8, 1024, 2 * LANES), jnp.bfloat16),
            pltpu.VMEM((16, columns, LANES), jnp.bfloat16),
            dma((5,)), dma((2,)), dma(parts), dma(parts), dma(parts), dma(parts),
            dma((15, PIECES)), dma((15, PIECES)),
        ],
        compiler_params=pltpu.CompilerParams(
            collective_id=0, has_side_effects=True, vmem_limit_bytes=40 * 2**20
        ),
    )(*(
        pltpu.with_memory_space_constraint(a, pltpu.HBM)
        for a in (offsets.T, strain, injections, filters, recon)
    ))


def pick_kernel(slots, pairs, out, even, odd, sem):
    width = even.shape[0]
    count = slots.shape[0] // width
    held = (even, odd)

    def fetch(c, b):
        lines = pl.ds(pl.multiple_of(c * width, width), width)
        return pltpu.make_async_copy(slots.at[lines], held[b], sem.at[b])

    for b in range(2):
        fetch(b, b).start()

    def step(i, carry):
        for b in range(2):
            c = 2 * i + b
            fetch(c, b).wait()
            base = c * width
            for u in range(width):
                out[base + u] = pairs[held[b][u]]

            @pl.when(c + 2 < count)
            def _():
                fetch(c + 2, b).start()
        return carry

    lax.fori_loop(0, count // 2, step, 0)


def turn_kernel(picked, out, select, spread):
    @pl.when(pl.program_id(0) == 0)
    def _():
        select[...] = pair_select(jnp.bfloat16)
        row = lax.broadcasted_iota(jnp.int32, (256, 256), 0)
        col = lax.broadcasted_iota(jnp.int32, (256, 256), 1)
        spread[...] = ((row // 16 == col % 16) & (row % 16 == col // 16)).astype(jnp.bfloat16)

    for g in range(picked.shape[0] // 2048):
        tiles = []
        for j in range(8):
            tiles.append(lax.dot_general(
                picked[pl.ds((8 * g + j) * 256, 256), :], select[...], (((0,), (0,)), ((), ())),
                preferred_element_type=jnp.float32,
            ).astype(jnp.bfloat16))
        for t in range(0, 8, 2):
            sides = [
                jnp.concatenate(
                    [tiles[j][16 * u:16 * u + 16, 128 * q:128 * q + 128]
                     for j in range(8) for q in range(2)],
                    axis=0,
                )
                for u in (t, t + 1)
            ]
            mixed = jnp.dot(
                spread[...], jnp.concatenate(sides, axis=1), preferred_element_type=jnp.float32
            ).astype(jnp.bfloat16)
            for h in range(2):
                out[pl.ds(16 * (t + h), 16), pl.ds(16 * g, 16), :] = (
                    mixed[:, 128 * h:128 * h + 128].reshape(16, 16, LANES)
                )


def put_in_order(slot_of, arrived):
    count = slot_of.shape[0]
    width, step = 1024, 2048
    vmem = pl.BlockSpec(memory_space=pltpu.VMEM)
    picked = pl.pallas_call(
        pick_kernel,
        out_shape=jax.ShapeDtypeStruct((count, 2, LANES), jnp.bfloat16),
        in_specs=[pl.BlockSpec(memory_space=pl.ANY), vmem],
        out_specs=vmem,
        scratch_shapes=[pltpu.SMEM((width,), jnp.int32)] * 2 + [pltpu.SemaphoreType.DMA((2,))],
        compiler_params=pltpu.CompilerParams(vmem_limit_bytes=40 * 2**20),
    )(slot_of, arrived.reshape(count, 2, LANES))
    tiles = count // LANES
    turned = pl.pallas_call(
        turn_kernel,
        out_shape=jax.ShapeDtypeStruct((2 * BLOCK, 2 * tiles, LANES), jnp.bfloat16),
        grid=(count // step,),
        in_specs=[pl.BlockSpec((2 * step, LANES), lambda i: (i, 0))],
        out_specs=pl.BlockSpec((2 * BLOCK, step // BLOCK, LANES), lambda i: (0, i, 0)),
        scratch_shapes=[pltpu.VMEM((256, 256), jnp.bfloat16)] * 2,
        compiler_params=pltpu.CompilerParams(vmem_limit_bytes=40 * 2**20),
    )(picked.reshape(2 * count, LANES))
    turned = turned.reshape(2 * BLOCK, tiles, 2, LANES).transpose(0, 2, 1, 3)
    return turned.reshape(2, BLOCK, 2, count)


def per_device(strain, injections, offsets, slot_of, basis_filters, recon_matrix):
    arrived = filter_and_exchange(strain, injections, offsets, basis_filters, recon_matrix)
    return put_in_order(slot_of, arrived)


def solution(mesh):
    return jax.shard_map(
        per_device,
        mesh=mesh,
        in_specs=(
            P(None, "tm"), P(), P(), P(),
            P("bank", "cuts", None, None), P("bank", "cuts", None, None),
        ),
        out_specs=P(None, ("tm", "bank", "cuts"), None, None),
        check_vma=False,
    )
```

```python
import functools

import jax
import jax.numpy as jnp
from jax import lax
from jax.experimental import pallas as pl
from jax.experimental.pallas import tpu as pltpu
from jax.sharding import PartitionSpec as P

MESH = pl.DeviceIdType.MESH
LANES = 128
BLOCK = 64
PIECES = 4
EARLY = 1
ORDER = (
    (2, 1), (2, 3), (1, 2), (3, 2),
    (2, 2), (2, 0), (0, 2),
    (1, 1), (3, 3), (1, 3), (3, 1),
    (1, 0), (3, 0), (0, 1), (0, 3),
)


def pair_select(dtype):
    row = lax.broadcasted_iota(jnp.int32, (256, 256), 0)
    col = lax.broadcasted_iota(jnp.int32, (256, 256), 1)
    return ((row // 2 == col % LANES) & (row % 2 == col // LANES)).astype(dtype)


def filter_kernel(
    offsets, strain, injections, filters, recon, out,
    places, spans, waves, windows, history, taps, raw, weights, basis, staged,
    local_sem, halo_sem, send_sem, recv_sem, pass_sem, got_sem, out_sem, in_sem,
):
    tm, bank, cuts = lax.axis_index("tm"), lax.axis_index("bank"), lax.axis_index("cuts")
    hi, core = tm // 2, tm % 2
    x, z = bank // 4, bank % 4
    partner = {"tm": hi * 2 + 1 - core}
    beside = ({"cuts": 1 - cuts}, {"tm": (1 - hi) * 2 + core, "cuts": 1 - cuts})
    after, before = {"tm": (tm + 1) % 4}, {"tm": (tm + 3) % 4}
    other = 4 * (1 - cuts)

    barrier = pltpu.get_barrier_semaphore()
    for device in (*beside, after, before, *({"bank": (bank + k) % 16} for k in range(1, 16))):
        pl.semaphore_signal(barrier, inc=1, device_id=device, device_id_type=MESH)

    locals_ = [
        pltpu.make_async_copy(strain, spans.at[1], local_sem.at[0]),
        pltpu.make_async_copy(injections, waves, local_sem.at[1]),
        pltpu.make_async_copy(recon.at[0], raw.at[pl.ds(4 * cuts, 4)], local_sem.at[2]),
        pltpu.make_async_copy(filters.at[0], taps.at[pl.ds(4 * cuts, 4)], local_sem.at[3]),
        pltpu.make_async_copy(offsets, places, local_sem.at[4]),
    ]
    for copy in locals_:
        copy.start()
    pl.semaphore_wait(barrier, 19)

    def part(n, source, slot):
        if n == 0:
            return (filters.at[0] if source else taps).at[slot]
        h, q = (n - 1) // 2, (n - 1) % 2
        return (recon.at[0] if source else raw).at[slot, :, pl.ds(512 * q + 128 * h, 128)]

    halo = pltpu.make_async_remote_copy(
        strain, spans.at[0], halo_sem.at[0], halo_sem.at[1],
        device_id=after, device_id_type=MESH,
    )
    halo.start()
    sends, passes = {}, {}
    for n in range(1 + 2 * PIECES):
        for j in range(2):
            mine = 2 * core + j
            sends[n, j] = pltpu.make_async_remote_copy(
                part(n, True, mine), part(n, False, 4 * cuts + mine),
                send_sem.at[j, n], recv_sem.at[j, n],
                device_id=beside[j], device_id_type=MESH,
            )
            sends[n, j].start()
            held = part(n, False, other + mine)
            passes[n, j] = pltpu.make_async_remote_copy(
                held, held, pass_sem.at[j, n], got_sem.at[j, n],
                device_id=partner, device_id_type=MESH,
            )

    def pass_on(parts):
        for n in parts:
            for j in range(2):
                sends[n, j].wait_recv()
                passes[n, j].start()

    locals_[0].wait()
    locals_[1].wait()
    locals_[4].wait()
    halo.wait()

    lane = lax.broadcasted_iota(jnp.int32, (32, LANES), 1)
    row32 = lax.broadcasted_iota(jnp.int32, (32, LANES), 0)
    low = lane < BLOCK
    known = (row32 >= 16) | (tm > 0)
    first_lane = lax.broadcasted_iota(jnp.int32, (1, LANES), 1)
    none = jnp.zeros((1, LANES), jnp.float32)
    for d in range(2):
        line = jnp.concatenate(
            [spans[r // 16, pl.ds(d, 1), pl.ds(LANES * (r % 16), LANES)] for r in range(32)], axis=0
        )
        for i in range(waves.shape[0]):
            first = places[d, i] - (tm - 1) * 2048
            row = first // LANES
            shift = first - row * LANES
            turned = [none] + [
                pltpu.roll(waves[i, pl.ds(d, 1), pl.ds(LANES * r, LANES)], shift, axis=1)
                for r in range(4)
            ] + [none]
            for r in range(5):
                placed = jnp.where(first_lane >= shift, turned[r + 1], turned[r])
                line += jnp.where(row32 == row + r, placed, 0.0)
        line = jnp.where(known, line, 0.0).astype(jnp.bfloat16).astype(jnp.float32)
        swapped = pltpu.roll(line, BLOCK, axis=1)
        if d == 1:
            windows[0] = line
            windows[1] = jnp.where(low, swapped, pltpu.roll(swapped, 31, axis=0))
        else:
            windows[2] = swapped
            windows[3] = jnp.where(low, pltpu.roll(line, 31, axis=0), line)
    half = lax.broadcasted_iota(jnp.int32, (BLOCK, LANES), 1) < BLOCK

    def fill(j, carry):
        for odd in range(2):
            row = j if odd else j + cuts
            tile = 60 + cuts - 2 * j if odd else 61 - cuts - 2 * j
            sides = []
            for kind in (2 + odd, odd):
                wide = jnp.broadcast_to(windows[kind, pl.ds(row, 1), :], (BLOCK, LANES))
                sides.append(pltpu.roll(wide, 0, axis=1, stride=1, stride_axis=0))
            value = jnp.where(half, sides[0], sides[1]).astype(jnp.bfloat16)
            history[pl.ds(pl.multiple_of(tile * BLOCK, BLOCK), BLOCK), :] = value
        return carry

    for j in range(31):
        fill(j, 0)

    select = pair_select(jnp.bfloat16)

    def turn(h, slot):
        pair = jnp.concatenate(
            [raw[slot, :, pl.ds(128 * h, 128)], raw[slot, :, pl.ds(512 + 128 * h, 128)]], axis=1
        )
        turned = lax.dot_general(
            select, pair, (((1,), (1,)), ((), ())), preferred_element_type=jnp.float32
        )
        where = pl.ds(pl.multiple_of(LANES * slot, LANES), LANES)
        weights[h, :, where] = turned.astype(jnp.bfloat16)

    def target_of(k):
        dx, dz = 0, 0
        for i, (a, b) in enumerate(ORDER):
            dx = jnp.where(k == i, a, dx)
            dz = jnp.where(k == i, b, dz)
        return ((x + dx) % 4) * 4 + (z + dz) % 4

    rows = weights.shape[1]

    def piece(k, h):
        lines = pl.ds(h * rows, rows)
        return pltpu.make_async_remote_copy(
            staged.at[k, lines], out.at[bank, lines], out_sem.at[k, h], in_sem.at[k, h],
            device_id={"bank": target_of(k)}, device_id_type=MESH,
        )

    def make_basis(i):
        starts = [LANES * (15 - target_of(2 * i + b)) for b in range(2)]
        for s in range(8):
            past = jnp.concatenate(
                [history[pl.ds(pl.multiple_of(p + 256 * s, LANES), 256), :] for p in starts],
                axis=1,
            )
            made = lax.dot_general(
                taps[s], past, (((0,), (0,)), ((), ())), preferred_element_type=jnp.float32
            )
            basis[i, pl.ds(LANES * s, LANES), :] = made.astype(jnp.bfloat16)

    def early(i, carry):
        make_basis(i)
        return carry

    def two_blocks(h, i, carry):
        if h == 0:
            @pl.when(i >= EARLY)
            def _():
                make_basis(i)
        made = jnp.dot(weights[h], basis[i], preferred_element_type=jnp.float32)
        made = made.astype(jnp.bfloat16)
        for b in range(2):
            staged[2 * i + b, pl.ds(h * rows, rows), :] = made[:, LANES * b:LANES * (b + 1)]
        piece(2 * i, h).start()

        @pl.when(i < 7)
        def _():
            piece(2 * i + 1, h).start()

        if h + 1 < PIECES:
            @pl.when(i == 3)
            def _():
                pass_on((3 + 2 * h, 4 + 2 * h))
        return carry

    pass_on((0,))
    locals_[2].wait()
    locals_[3].wait()
    for i in range(4):
        turn(0, 4 * cuts + i)
    for j in range(2):
        passes[0, j].wait_recv()
    lax.fori_loop(0, EARLY, early, 0)
    pass_on((1, 2))
    for i in range(2):
        turn(0, other + 2 * core + i)
    for h in range(PIECES):
        for n in (1 + 2 * h, 2 + 2 * h):
            for j in range(2):
                passes[n, j].wait_recv()
        if h == 0:
            for i in range(2):
                turn(0, other + 2 * (1 - core) + i)
        else:
            for i in range(8):
                turn(h, i)
        lax.fori_loop(0, 8, functools.partial(two_blocks, h), 0)
    own = pltpu.make_async_copy(staged.at[15], out.at[bank], local_sem.at[0])
    own.start()

    def finish(k, carry):
        for h in range(PIECES):
            copy = piece(k, h)
            copy.wait_send()
            copy.wait_recv()
        return carry

    lax.fori_loop(0, 15, finish, 0)
    own.wait()
    for copy in (*sends.values(), *passes.values()):
        copy.wait_send()


def filter_and_exchange(strain, injections, offsets, filters, recon):
    hbm = pl.BlockSpec(memory_space=pltpu.HBM)
    columns = recon.shape[3]
    dma = pltpu.SemaphoreType.DMA
    parts = (2, 1 + 2 * PIECES)
    return pl.pallas_call(
        filter_kernel,
        out_shape=jax.ShapeDtypeStruct((16, columns, LANES), jnp.bfloat16),
        in_specs=[hbm] * 5,
        out_specs=pl.BlockSpec(memory_space=pl.ANY),
        scratch_shapes=[
            pltpu.SMEM(offsets.shape[::-1], jnp.int32),
            pltpu.VMEM((2, *strain.shape), jnp.float32),
            pltpu.VMEM(injections.shape, jnp.float32),
            pltpu.VMEM((4, 32, LANES), jnp.float32),
            pltpu.VMEM((62 * BLOCK, LANES), jnp.bfloat16),
            pltpu.VMEM((8, 256, 128), jnp.bfloat16),
            pltpu.VMEM((8, 128, columns), jnp.bfloat16),
            pltpu.VMEM((PIECES, columns // PIECES, 1024), jnp.bfloat16),
            pltpu.VMEM((8, 1024, 2 * LANES), jnp.bfloat16),
            pltpu.VMEM((16, columns, LANES), jnp.bfloat16),
            dma((5,)), dma((2,)), dma(parts), dma(parts), dma(parts), dma(parts),
            dma((15, PIECES)), dma((15, PIECES)),
        ],
        compiler_params=pltpu.CompilerParams(
            collective_id=0, has_side_effects=True, vmem_limit_bytes=40 * 2**20
        ),
    )(*(
        pltpu.with_memory_space_constraint(a, pltpu.HBM)
        for a in (offsets.T, strain, injections, filters, recon)
    ))


def pick_kernel(slots, pairs, out, even, odd, sem):
    width = even.shape[0]
    count = slots.shape[0] // width
    held = (even, odd)

    def fetch(c, b):
        lines = pl.ds(pl.multiple_of(c * width, width), width)
        return pltpu.make_async_copy(slots.at[lines], held[b], sem.at[b])

    for b in range(2):
        fetch(b, b).start()

    def step(i, carry):
        for b in range(2):
            c = 2 * i + b
            fetch(c, b).wait()
            base = c * width
            for u in range(width):
                out[base + u] = pairs[held[b][u]]

            @pl.when(c + 2 < count)
            def _():
                fetch(c + 2, b).start()
        return carry

    lax.fori_loop(0, count // 2, step, 0)


def turn_kernel(picked, out, select, spread):
    @pl.when(pl.program_id(0) == 0)
    def _():
        select[...] = pair_select(jnp.bfloat16)
        row = lax.broadcasted_iota(jnp.int32, (256, 256), 0)
        col = lax.broadcasted_iota(jnp.int32, (256, 256), 1)
        spread[...] = ((row // 16 == col % 16) & (row % 16 == col // 16)).astype(jnp.bfloat16)

    def tile(g, j):
        return lax.dot_general(
            picked[pl.ds((8 * g + j) * 256, 256), :], select[...], (((0,), (0,)), ((), ())),
            preferred_element_type=jnp.float32,
        ).astype(jnp.bfloat16)

    def finish(g, tiles, t):
        sides = [
            jnp.concatenate(
                [tiles[j][16 * u:16 * u + 16, 128 * q:128 * q + 128]
                 for j in range(8) for q in range(2)],
                axis=0,
            )
            for u in (t, t + 1)
        ]
        mixed = jnp.dot(
            spread[...], jnp.concatenate(sides, axis=1), preferred_element_type=jnp.float32
        ).astype(jnp.bfloat16)
        for h in range(2):
            out[pl.ds(16 * (t + h), 16), pl.ds(16 * g, 16), :] = (
                mixed[:, 128 * h:128 * h + 128].reshape(16, 16, LANES)
            )

    groups = picked.shape[0] // 2048
    tiles = [tile(0, j) for j in range(8)]
    for g in range(groups):
        later = []
        for t in range(0, 8, 2):
            if g + 1 < groups:
                later.append(tile(g + 1, t))
            finish(g, tiles, t)
            if g + 1 < groups:
                later.append(tile(g + 1, t + 1))
        tiles = later


def put_in_order(slot_of, arrived):
    count = slot_of.shape[0]
    width, step = 1024, 4096
    vmem = pl.BlockSpec(memory_space=pltpu.VMEM)
    picked = pl.pallas_call(
        pick_kernel,
        out_shape=jax.ShapeDtypeStruct((count, 2, LANES), jnp.bfloat16),
        in_specs=[pl.BlockSpec(memory_space=pl.ANY), vmem],
        out_specs=vmem,
        scratch_shapes=[pltpu.SMEM((width,), jnp.int32)] * 2 + [pltpu.SemaphoreType.DMA((2,))],
        compiler_params=pltpu.CompilerParams(vmem_limit_bytes=40 * 2**20),
    )(slot_of, arrived.reshape(count, 2, LANES))
    tiles = count // LANES
    turned = pl.pallas_call(
        turn_kernel,
        out_shape=jax.ShapeDtypeStruct((2 * BLOCK, 2 * tiles, LANES), jnp.bfloat16),
        grid=(count // step,),
        in_specs=[pl.BlockSpec((2 * step, LANES), lambda i: (i, 0))],
        out_specs=pl.BlockSpec((2 * BLOCK, step // BLOCK, LANES), lambda i: (0, i, 0)),
        scratch_shapes=[pltpu.VMEM((256, 256), jnp.bfloat16)] * 2,
        compiler_params=pltpu.CompilerParams(vmem_limit_bytes=40 * 2**20),
    )(picked.reshape(2 * count, LANES))
    turned = turned.reshape(2 * BLOCK, tiles, 2, LANES).transpose(0, 2, 1, 3)
    return turned.reshape(2, BLOCK, 2, count)


def per_device(strain, injections, offsets, slot_of, basis_filters, recon_matrix):
    arrived = filter_and_exchange(strain, injections, offsets, basis_filters, recon_matrix)
    return put_in_order(slot_of, arrived)


def solution(mesh):
    return jax.shard_map(
        per_device,
        mesh=mesh,
        in_specs=(
            P(None, "tm"), P(), P(), P(),
            P("bank", "cuts", None, None), P("bank", "cuts", None, None),
        ),
        out_specs=P(None, ("tm", "bank", "cuts"), None, None),
        check_vma=False,
    )
```

```python
import functools

import jax
import jax.numpy as jnp
from jax import lax
from jax.experimental import pallas as pl
from jax.experimental.pallas import tpu as pltpu
from jax.sharding import PartitionSpec as P

MESH = pl.DeviceIdType.MESH
LANES = 128
BLOCK = 64
PIECES = 4
EARLY = 1
ORDER = (
    (2, 1), (2, 3), (1, 2), (3, 2),
    (2, 2), (2, 0), (0, 2),
    (1, 1), (3, 3), (1, 3), (3, 1),
    (1, 0), (3, 0), (0, 1), (0, 3),
)


def pair_select(dtype):
    row = lax.broadcasted_iota(jnp.int32, (256, 256), 0)
    col = lax.broadcasted_iota(jnp.int32, (256, 256), 1)
    return ((row // 2 == col % LANES) & (row % 2 == col // LANES)).astype(dtype)


def filter_kernel(
    offsets, strain, injections, filters, recon, out,
    places, spans, waves, windows, history, taps, raw, weights, basis, staged,
    local_sem, halo_sem, send_sem, recv_sem, pass_sem, got_sem, out_sem, in_sem,
):
    tm, bank, cuts = lax.axis_index("tm"), lax.axis_index("bank"), lax.axis_index("cuts")
    hi, core = tm // 2, tm % 2
    x, z = bank // 4, bank % 4
    partner = {"tm": hi * 2 + 1 - core}
    beside = ({"cuts": 1 - cuts}, {"tm": (1 - hi) * 2 + core, "cuts": 1 - cuts})
    after, before = {"tm": (tm + 1) % 4}, {"tm": (tm + 3) % 4}
    other = 4 * (1 - cuts)

    barrier = pltpu.get_barrier_semaphore()
    for device in (*beside, after, before, *({"bank": (bank + k) % 16} for k in range(1, 16))):
        pl.semaphore_signal(barrier, inc=1, device_id=device, device_id_type=MESH)

    locals_ = [
        pltpu.make_async_copy(strain, spans.at[1], local_sem.at[0]),
        pltpu.make_async_copy(injections, waves, local_sem.at[1]),
        pltpu.make_async_copy(recon.at[0], raw.at[pl.ds(4 * cuts, 4)], local_sem.at[2]),
        pltpu.make_async_copy(filters.at[0], taps.at[pl.ds(4 * cuts, 4)], local_sem.at[3]),
        pltpu.make_async_copy(offsets, places, local_sem.at[4]),
    ]
    for copy in locals_:
        copy.start()
    pl.semaphore_wait(barrier, 19)

    def part(n, source, slot):
        if n == 0:
            return (filters.at[0] if source else taps).at[slot]
        h, q = (n - 1) // 2, (n - 1) % 2
        return (recon.at[0] if source else raw).at[slot, :, pl.ds(512 * q + 128 * h, 128)]

    halo = pltpu.make_async_remote_copy(
        strain, spans.at[0], halo_sem.at[0], halo_sem.at[1],
        device_id=after, device_id_type=MESH,
    )
    halo.start()
    sends, passes = {}, {}
    for n in range(1 + 2 * PIECES):
        for j in range(2):
            mine = 2 * core + j
            sends[n, j] = pltpu.make_async_remote_copy(
                part(n, True, mine), part(n, False, 4 * cuts + mine),
                send_sem.at[j, n], recv_sem.at[j, n],
                device_id=beside[j], device_id_type=MESH,
            )
            sends[n, j].start()
            held = part(n, False, other + mine)
            passes[n, j] = pltpu.make_async_remote_copy(
                held, held, pass_sem.at[j, n], got_sem.at[j, n],
                device_id=partner, device_id_type=MESH,
            )

    def pass_on(parts):
        for n in parts:
            for j in range(2):
                sends[n, j].wait_recv()
                passes[n, j].start()

    locals_[0].wait()
    locals_[1].wait()
    locals_[4].wait()
    halo.wait()

    lane = lax.broadcasted_iota(jnp.int32, (32, LANES), 1)
    row32 = lax.broadcasted_iota(jnp.int32, (32, LANES), 0)
    low = lane < BLOCK
    known = (row32 >= 16) | (tm > 0)
    first_lane = lax.broadcasted_iota(jnp.int32, (1, LANES), 1)
    none = jnp.zeros((1, LANES), jnp.float32)
    for d in range(2):
        line = jnp.concatenate(
            [spans[r // 16, pl.ds(d, 1), pl.ds(LANES * (r % 16), LANES)] for r in range(32)], axis=0
        )
        for i in range(waves.shape[0]):
            first = places[d, i] - (tm - 1) * 2048
            row = first // LANES
            shift = first - row * LANES
            turned = [none] + [
                pltpu.roll(waves[i, pl.ds(d, 1), pl.ds(LANES * r, LANES)], shift, axis=1)
                for r in range(4)
            ] + [none]
            for r in range(5):
                placed = jnp.where(first_lane >= shift, turned[r + 1], turned[r])
                line += jnp.where(row32 == row + r, placed, 0.0)
        line = jnp.where(known, line, 0.0).astype(jnp.bfloat16).astype(jnp.float32)
        swapped = pltpu.roll(line, BLOCK, axis=1)
        if d == 1:
            windows[0] = line
            windows[1] = jnp.where(low, swapped, pltpu.roll(swapped, 31, axis=0))
        else:
            windows[2] = swapped
            windows[3] = jnp.where(low, pltpu.roll(line, 31, axis=0), line)
    half = lax.broadcasted_iota(jnp.int32, (BLOCK, LANES), 1) < BLOCK

    def fill(j, carry):
        for odd in range(2):
            row = j if odd else j + cuts
            tile = 60 + cuts - 2 * j if odd else 61 - cuts - 2 * j
            sides = []
            for kind in (2 + odd, odd):
                wide = jnp.broadcast_to(windows[kind, pl.ds(row, 1), :], (BLOCK, LANES))
                sides.append(pltpu.roll(wide, 0, axis=1, stride=1, stride_axis=0))
            value = jnp.where(half, sides[0], sides[1]).astype(jnp.bfloat16)
            history[pl.ds(pl.multiple_of(tile * BLOCK, BLOCK), BLOCK), :] = value
        return carry

    for j in range(31):
        fill(j, 0)

    select = pair_select(jnp.bfloat16)

    def turn(h, slot):
        pair = jnp.concatenate(
            [raw[slot, :, pl.ds(128 * h, 128)], raw[slot, :, pl.ds(512 + 128 * h, 128)]], axis=1
        )
        turned = lax.dot_general(
            select, pair, (((1,), (1,)), ((), ())), preferred_element_type=jnp.float32
        )
        where = pl.ds(pl.multiple_of(LANES * slot, LANES), LANES)
        weights[h, :, where] = turned.astype(jnp.bfloat16)

    def target_of(k):
        dx, dz = 0, 0
        for i, (a, b) in enumerate(ORDER):
            dx = jnp.where(k == i, a, dx)
            dz = jnp.where(k == i, b, dz)
        dx, dz = jnp.where(core == 1, dz, dx), jnp.where(core == 1, dx, dz)
        return ((x + dx) % 4) * 4 + (z + dz) % 4

    rows = weights.shape[1]

    def piece(k, h):
        lines = pl.ds(h * rows, rows)
        return pltpu.make_async_remote_copy(
            staged.at[k, lines], out.at[bank, lines], out_sem.at[k, h], in_sem.at[k, h],
            device_id={"bank": target_of(k)}, device_id_type=MESH,
        )

    def make_basis(i):
        starts = [LANES * (15 - target_of(2 * i + b)) for b in range(2)]
        for s in range(8):
            past = jnp.concatenate(
                [history[pl.ds(pl.multiple_of(p + 256 * s, LANES), 256), :] for p in starts],
                axis=1,
            )
            made = lax.dot_general(
                taps[s], past, (((0,), (0,)), ((), ())), preferred_element_type=jnp.float32
            )
            basis[i, pl.ds(LANES * s, LANES), :] = made.astype(jnp.bfloat16)

    def early(i, carry):
        make_basis(i)
        return carry

    def two_blocks(h, i, carry):
        if h == 0:
            @pl.when(i >= EARLY)
            def _():
                make_basis(i)
        made = jnp.dot(weights[h], basis[i], preferred_element_type=jnp.float32)
        made = made.astype(jnp.bfloat16)
        for b in range(2):
            staged[2 * i + b, pl.ds(h * rows, rows), :] = made[:, LANES * b:LANES * (b + 1)]
        piece(2 * i, h).start()

        @pl.when(i < 7)
        def _():
            piece(2 * i + 1, h).start()

        if h + 1 < PIECES:
            @pl.when(i == 3)
            def _():
                pass_on((3 + 2 * h, 4 + 2 * h))
        return carry

    pass_on((0,))
    locals_[2].wait()
    locals_[3].wait()
    for i in range(4):
        turn(0, 4 * cuts + i)
    for j in range(2):
        passes[0, j].wait_recv()
    lax.fori_loop(0, EARLY, early, 0)
    pass_on((1, 2))
    for i in range(2):
        turn(0, other + 2 * core + i)
    for h in range(PIECES):
        for n in (1 + 2 * h, 2 + 2 * h):
            for j in range(2):
                passes[n, j].wait_recv()
        if h == 0:
            for i in range(2):
                turn(0, other + 2 * (1 - core) + i)
        else:
            for i in range(8):
                turn(h, i)
        lax.fori_loop(0, 8, functools.partial(two_blocks, h), 0)
    own = pltpu.make_async_copy(staged.at[15], out.at[bank], local_sem.at[0])
    own.start()

    def finish(k, carry):
        for h in range(PIECES):
            copy = piece(k, h)
            copy.wait_send()
            copy.wait_recv()
        return carry

    lax.fori_loop(0, 15, finish, 0)
    own.wait()
    for copy in (*sends.values(), *passes.values()):
        copy.wait_send()


def filter_and_exchange(strain, injections, offsets, filters, recon):
    hbm = pl.BlockSpec(memory_space=pltpu.HBM)
    columns = recon.shape[3]
    dma = pltpu.SemaphoreType.DMA
    parts = (2, 1 + 2 * PIECES)
    return pl.pallas_call(
        filter_kernel,
        out_shape=jax.ShapeDtypeStruct((16, columns, LANES), jnp.bfloat16),
        in_specs=[hbm] * 5,
        out_specs=pl.BlockSpec(memory_space=pl.ANY),
        scratch_shapes=[
            pltpu.SMEM(offsets.shape[::-1], jnp.int32),
            pltpu.VMEM((2, *strain.shape), jnp.float32),
            pltpu.VMEM(injections.shape, jnp.float32),
            pltpu.VMEM((4, 32, LANES), jnp.float32),
            pltpu.VMEM((62 * BLOCK, LANES), jnp.bfloat16),
            pltpu.VMEM((8, 256, 128), jnp.bfloat16),
            pltpu.VMEM((8, 128, columns), jnp.bfloat16),
            pltpu.VMEM((PIECES, columns // PIECES, 1024), jnp.bfloat16),
            pltpu.VMEM((8, 1024, 2 * LANES), jnp.bfloat16),
            pltpu.VMEM((16, columns, LANES), jnp.bfloat16),
            dma((5,)), dma((2,)), dma(parts), dma(parts), dma(parts), dma(parts),
            dma((15, PIECES)), dma((15, PIECES)),
        ],
        compiler_params=pltpu.CompilerParams(
            collective_id=0, has_side_effects=True, vmem_limit_bytes=40 * 2**20
        ),
    )(*(
        pltpu.with_memory_space_constraint(a, pltpu.HBM)
        for a in (offsets.T, strain, injections, filters, recon)
    ))


def pick_kernel(slots, pairs, out, even, odd, sem):
    width = even.shape[0]
    count = slots.shape[0] // width
    held = (even, odd)

    def fetch(c, b):
        lines = pl.ds(pl.multiple_of(c * width, width), width)
        return pltpu.make_async_copy(slots.at[lines], held[b], sem.at[b])

    for b in range(2):
        fetch(b, b).start()

    def step(i, carry):
        for b in range(2):
            c = 2 * i + b
            fetch(c, b).wait()
            base = c * width
            for u in range(width):
                out[base + u] = pairs[held[b][u]]

            @pl.when(c + 2 < count)
            def _():
                fetch(c + 2, b).start()
        return carry

    lax.fori_loop(0, count // 2, step, 0)


def turn_kernel(picked, out, select, spread):
    @pl.when(pl.program_id(0) == 0)
    def _():
        select[...] = pair_select(jnp.bfloat16)
        row = lax.broadcasted_iota(jnp.int32, (256, 256), 0)
        col = lax.broadcasted_iota(jnp.int32, (256, 256), 1)
        spread[...] = ((row // 16 == col % 16) & (row % 16 == col // 16)).astype(jnp.bfloat16)

    def tile(g, j):
        return lax.dot_general(
            picked[pl.ds((8 * g + j) * 256, 256), :], select[...], (((0,), (0,)), ((), ())),
            preferred_element_type=jnp.float32,
        ).astype(jnp.bfloat16)

    def finish(g, tiles, t):
        sides = [
            jnp.concatenate(
                [tiles[j][16 * u:16 * u + 16, 128 * q:128 * q + 128]
                 for j in range(8) for q in range(2)],
                axis=0,
            )
            for u in (t, t + 1)
        ]
        mixed = jnp.dot(
            spread[...], jnp.concatenate(sides, axis=1), preferred_element_type=jnp.float32
        ).astype(jnp.bfloat16)
        for h in range(2):
            out[pl.ds(16 * (t + h), 16), pl.ds(16 * g, 16), :] = (
                mixed[:, 128 * h:128 * h + 128].reshape(16, 16, LANES)
            )

    groups = picked.shape[0] // 2048
    tiles = [tile(0, j) for j in range(8)]
    for g in range(groups):
        later = []
        for t in range(0, 8, 2):
            if g + 1 < groups:
                later.append(tile(g + 1, t))
            finish(g, tiles, t)
            if g + 1 < groups:
                later.append(tile(g + 1, t + 1))
        tiles = later


def put_in_order(slot_of, arrived):
    count = slot_of.shape[0]
    width, step = 1024, 4096
    vmem = pl.BlockSpec(memory_space=pltpu.VMEM)
    picked = pl.pallas_call(
        pick_kernel,
        out_shape=jax.ShapeDtypeStruct((count, 2, LANES), jnp.bfloat16),
        in_specs=[pl.BlockSpec(memory_space=pl.ANY), vmem],
        out_specs=vmem,
        scratch_shapes=[pltpu.SMEM((width,), jnp.int32)] * 2 + [pltpu.SemaphoreType.DMA((2,))],
        compiler_params=pltpu.CompilerParams(vmem_limit_bytes=40 * 2**20),
    )(slot_of, arrived.reshape(count, 2, LANES))
    tiles = count // LANES
    turned = pl.pallas_call(
        turn_kernel,
        out_shape=jax.ShapeDtypeStruct((2 * BLOCK, 2 * tiles, LANES), jnp.bfloat16),
        grid=(count // step,),
        in_specs=[pl.BlockSpec((2 * step, LANES), lambda i: (i, 0))],
        out_specs=pl.BlockSpec((2 * BLOCK, step // BLOCK, LANES), lambda i: (0, i, 0)),
        scratch_shapes=[pltpu.VMEM((256, 256), jnp.bfloat16)] * 2,
        compiler_params=pltpu.CompilerParams(vmem_limit_bytes=40 * 2**20),
    )(picked.reshape(2 * count, LANES))
    turned = turned.reshape(2 * BLOCK, tiles, 2, LANES).transpose(0, 2, 1, 3)
    return turned.reshape(2, BLOCK, 2, count)


def per_device(strain, injections, offsets, slot_of, basis_filters, recon_matrix):
    arrived = filter_and_exchange(strain, injections, offsets, basis_filters, recon_matrix)
    return put_in_order(slot_of, arrived)


def solution(mesh):
    return jax.shard_map(
        per_device,
        mesh=mesh,
        in_specs=(
            P(None, "tm"), P(), P(), P(),
            P("bank", "cuts", None, None), P("bank", "cuts", None, None),
        ),
        out_specs=P(None, ("tm", "bank", "cuts"), None, None),
        check_vma=False,
    )
```

```python
import functools

import jax
import jax.numpy as jnp
from jax import lax
from jax.experimental import pallas as pl
from jax.experimental.pallas import tpu as pltpu
from jax.sharding import PartitionSpec as P

MESH = pl.DeviceIdType.MESH
LANES = 128
BLOCK = 64
PIECES = 4
EARLY = 1
ORDER = (
    (2, 1), (2, 3), (1, 2), (3, 2),
    (2, 2), (2, 0), (0, 2),
    (1, 1), (3, 3), (1, 3), (3, 1),
    (1, 0), (3, 0), (0, 1), (0, 3),
)


def pair_select(dtype):
    row = lax.broadcasted_iota(jnp.int32, (256, 256), 0)
    col = lax.broadcasted_iota(jnp.int32, (256, 256), 1)
    return ((row // 2 == col % LANES) & (row % 2 == col // LANES)).astype(dtype)


def filter_kernel(
    offsets, strain, injections, filters, recon, out,
    places, spans, waves, windows, history, taps, raw, weights, basis, staged,
    local_sem, halo_sem, send_sem, recv_sem, pass_sem, got_sem, out_sem, in_sem,
):
    tm, bank, cuts = lax.axis_index("tm"), lax.axis_index("bank"), lax.axis_index("cuts")
    hi, core = tm // 2, tm % 2
    x, z = bank // 4, bank % 4
    partner = {"tm": hi * 2 + 1 - core}
    beside = ({"cuts": 1 - cuts}, {"tm": (1 - hi) * 2 + core, "cuts": 1 - cuts})
    after, before = {"tm": (tm + 1) % 4}, {"tm": (tm + 3) % 4}
    other = 4 * (1 - cuts)

    barrier = pltpu.get_barrier_semaphore()
    for device in (*beside, after, before, *({"bank": (bank + k) % 16} for k in range(1, 16))):
        pl.semaphore_signal(barrier, inc=1, device_id=device, device_id_type=MESH)

    locals_ = [
        pltpu.make_async_copy(strain, spans.at[1], local_sem.at[0]),
        pltpu.make_async_copy(injections, waves, local_sem.at[1]),
        pltpu.make_async_copy(recon.at[0], raw.at[pl.ds(4 * cuts, 4)], local_sem.at[2]),
        pltpu.make_async_copy(filters.at[0], taps.at[pl.ds(4 * cuts, 4)], local_sem.at[3]),
        pltpu.make_async_copy(offsets, places, local_sem.at[4]),
    ]
    for copy in locals_:
        copy.start()
    pl.semaphore_wait(barrier, 19)

    def part(n, source, slot):
        if n == 0:
            return (filters.at[0] if source else taps).at[slot]
        h, q = (n - 1) // 2, (n - 1) % 2
        return (recon.at[0] if source else raw).at[slot, :, pl.ds(512 * q + 128 * h, 128)]

    halo = pltpu.make_async_remote_copy(
        strain, spans.at[0], halo_sem.at[0], halo_sem.at[1],
        device_id=after, device_id_type=MESH,
    )
    halo.start()
    sends, passes = {}, {}
    for n in range(1 + 2 * PIECES):
        for j in range(2):
            mine = 2 * core + j
            sends[n, j] = pltpu.make_async_remote_copy(
                part(n, True, mine), part(n, False, 4 * cuts + mine),
                send_sem.at[j, n], recv_sem.at[j, n],
                device_id=beside[j], device_id_type=MESH,
            )
            sends[n, j].start()
            held = part(n, False, other + mine)
            passes[n, j] = pltpu.make_async_remote_copy(
                held, held, pass_sem.at[j, n], got_sem.at[j, n],
                device_id=partner, device_id_type=MESH,
            )

    def pass_on(parts):
        for n in parts:
            for j in range(2):
                sends[n, j].wait_recv()
                passes[n, j].start()

    locals_[0].wait()
    locals_[1].wait()
    locals_[4].wait()
    halo.wait()

    lane = lax.broadcasted_iota(jnp.int32, (32, LANES), 1)
    row32 = lax.broadcasted_iota(jnp.int32, (32, LANES), 0)
    low = lane < BLOCK
    known = (row32 >= 16) | (tm > 0)
    first_lane = lax.broadcasted_iota(jnp.int32, (1, LANES), 1)
    none = jnp.zeros((1, LANES), jnp.float32)
    for d in range(2):
        line = jnp.concatenate(
            [spans[r // 16, pl.ds(d, 1), pl.ds(LANES * (r % 16), LANES)] for r in range(32)], axis=0
        )
        for i in range(waves.shape[0]):
            first = places[d, i] - (tm - 1) * 2048
            row = first // LANES
            shift = first - row * LANES
            turned = [none] + [
                pltpu.roll(waves[i, pl.ds(d, 1), pl.ds(LANES * r, LANES)], shift, axis=1)
                for r in range(4)
            ] + [none]
            for r in range(5):
                placed = jnp.where(first_lane >= shift, turned[r + 1], turned[r])
                line += jnp.where(row32 == row + r, placed, 0.0)
        line = jnp.where(known, line, 0.0).astype(jnp.bfloat16).astype(jnp.float32)
        swapped = pltpu.roll(line, BLOCK, axis=1)
        if d == 1:
            windows[0] = line
            windows[1] = jnp.where(low, swapped, pltpu.roll(swapped, 31, axis=0))
        else:
            windows[2] = swapped
            windows[3] = jnp.where(low, pltpu.roll(line, 31, axis=0), line)
    half = lax.broadcasted_iota(jnp.int32, (BLOCK, LANES), 1) < BLOCK

    def fill(j, carry):
        for odd in range(2):
            row = j if odd else j + cuts
            tile = 60 + cuts - 2 * j if odd else 61 - cuts - 2 * j
            sides = []
            for kind in (2 + odd, odd):
                wide = jnp.broadcast_to(windows[kind, pl.ds(row, 1), :], (BLOCK, LANES))
                sides.append(pltpu.roll(wide, 0, axis=1, stride=1, stride_axis=0))
            value = jnp.where(half, sides[0], sides[1]).astype(jnp.bfloat16)
            history[pl.ds(pl.multiple_of(tile * BLOCK, BLOCK), BLOCK), :] = value
        return carry

    for j in range(31):
        fill(j, 0)

    select = pair_select(jnp.bfloat16)

    def turn(h, slot):
        pair = jnp.concatenate(
            [raw[slot, :, pl.ds(128 * h, 128)], raw[slot, :, pl.ds(512 + 128 * h, 128)]], axis=1
        )
        turned = lax.dot_general(
            select, pair, (((1,), (1,)), ((), ())), preferred_element_type=jnp.float32
        )
        where = pl.ds(pl.multiple_of(LANES * slot, LANES), LANES)
        weights[h, :, where] = turned.astype(jnp.bfloat16)

    def target_of(k):
        dx, dz = 0, 0
        for i, (a, b) in enumerate(ORDER):
            dx = jnp.where(k == i, a, dx)
            dz = jnp.where(k == i, b, dz)
        dx, dz = jnp.where(core == 1, dz, dx), jnp.where(core == 1, dx, dz)
        return ((x + dx) % 4) * 4 + (z + dz) % 4

    rows = weights.shape[1]

    def piece(k, h):
        lines = pl.ds(h * rows, rows)
        return pltpu.make_async_remote_copy(
            staged.at[k, lines], out.at[bank, lines], out_sem.at[k, h], in_sem.at[k, h],
            device_id={"bank": target_of(k)}, device_id_type=MESH,
        )

    def make_basis(i):
        starts = [LANES * (15 - target_of(2 * i + b)) for b in range(2)]
        for s in range(8):
            past = jnp.concatenate(
                [history[pl.ds(pl.multiple_of(p + 256 * s, LANES), 256), :] for p in starts],
                axis=1,
            )
            made = lax.dot_general(
                taps[s], past, (((0,), (0,)), ((), ())), preferred_element_type=jnp.float32
            )
            basis[i, pl.ds(LANES * s, LANES), :] = made.astype(jnp.bfloat16)

    def early(i, carry):
        make_basis(i)
        return carry

    def two_blocks(h, i, carry):
        if h == 0:
            @pl.when(i >= EARLY)
            def _():
                make_basis(i)
        made = jnp.dot(weights[h], basis[i], preferred_element_type=jnp.float32)
        made = made.astype(jnp.bfloat16)
        for b in range(2):
            staged[2 * i + b, pl.ds(h * rows, rows), :] = made[:, LANES * b:LANES * (b + 1)]
        piece(2 * i, h).start()

        @pl.when(i < 7)
        def _():
            piece(2 * i + 1, h).start()

        if h + 1 < PIECES:
            @pl.when(i == 3)
            def _():
                pass_on((3 + 2 * h, 4 + 2 * h))
        return carry

    pass_on((0,))
    locals_[2].wait()
    locals_[3].wait()
    for i in range(4):
        turn(0, 4 * cuts + i)
    for j in range(2):
        passes[0, j].wait_recv()
    pass_on((1, 2))
    lax.fori_loop(0, EARLY, early, 0)
    for i in range(2):
        turn(0, other + 2 * core + i)
    for h in range(PIECES):
        for n in (1 + 2 * h, 2 + 2 * h):
            for j in range(2):
                passes[n, j].wait_recv()
        if h == 0:
            for i in range(2):
                turn(0, other + 2 * (1 - core) + i)
        else:
            for i in range(8):
                turn(h, i)
        lax.fori_loop(0, 8, functools.partial(two_blocks, h), 0)
    own = pltpu.make_async_copy(staged.at[15], out.at[bank], local_sem.at[0])
    own.start()

    def finish(k, carry):
        for h in range(PIECES):
            copy = piece(k, h)
            copy.wait_send()
            copy.wait_recv()
        return carry

    lax.fori_loop(0, 15, finish, 0)
    own.wait()
    for copy in (*sends.values(), *passes.values()):
        copy.wait_send()


def filter_and_exchange(strain, injections, offsets, filters, recon):
    hbm = pl.BlockSpec(memory_space=pltpu.HBM)
    columns = recon.shape[3]
    dma = pltpu.SemaphoreType.DMA
    parts = (2, 1 + 2 * PIECES)
    return pl.pallas_call(
        filter_kernel,
        out_shape=jax.ShapeDtypeStruct((16, columns, LANES), jnp.bfloat16),
        in_specs=[hbm] * 5,
        out_specs=pl.BlockSpec(memory_space=pl.ANY),
        scratch_shapes=[
            pltpu.SMEM(offsets.shape[::-1], jnp.int32),
            pltpu.VMEM((2, *strain.shape), jnp.float32),
            pltpu.VMEM(injections.shape, jnp.float32),
            pltpu.VMEM((4, 32, LANES), jnp.float32),
            pltpu.VMEM((62 * BLOCK, LANES), jnp.bfloat16),
            pltpu.VMEM((8, 256, 128), jnp.bfloat16),
            pltpu.VMEM((8, 128, columns), jnp.bfloat16),
            pltpu.VMEM((PIECES, columns // PIECES, 1024), jnp.bfloat16),
            pltpu.VMEM((8, 1024, 2 * LANES), jnp.bfloat16),
            pltpu.VMEM((16, columns, LANES), jnp.bfloat16),
            dma((5,)), dma((2,)), dma(parts), dma(parts), dma(parts), dma(parts),
            dma((15, PIECES)), dma((15, PIECES)),
        ],
        compiler_params=pltpu.CompilerParams(
            collective_id=0, has_side_effects=True, vmem_limit_bytes=40 * 2**20
        ),
    )(*(
        pltpu.with_memory_space_constraint(a, pltpu.HBM)
        for a in (offsets.T, strain, injections, filters, recon)
    ))


def pick_kernel(slots, pairs, out, even, odd, sem):
    width = even.shape[0]
    count = slots.shape[0] // width
    held = (even, odd)

    def fetch(c, b):
        lines = pl.ds(pl.multiple_of(c * width, width), width)
        return pltpu.make_async_copy(slots.at[lines], held[b], sem.at[b])

    for b in range(2):
        fetch(b, b).start()

    def step(i, carry):
        for b in range(2):
            c = 2 * i + b
            fetch(c, b).wait()
            base = c * width
            for u in range(width):
                out[base + u] = pairs[held[b][u]]

            @pl.when(c + 2 < count)
            def _():
                fetch(c + 2, b).start()
        return carry

    lax.fori_loop(0, count // 2, step, 0)


def turn_kernel(picked, out, select, spread):
    @pl.when(pl.program_id(0) == 0)
    def _():
        select[...] = pair_select(jnp.bfloat16)
        row = lax.broadcasted_iota(jnp.int32, (256, 256), 0)
        col = lax.broadcasted_iota(jnp.int32, (256, 256), 1)
        spread[...] = ((row // 16 == col % 16) & (row % 16 == col // 16)).astype(jnp.bfloat16)

    def tile(g, j):
        return lax.dot_general(
            picked[pl.ds((8 * g + j) * 256, 256), :], select[...], (((0,), (0,)), ((), ())),
            preferred_element_type=jnp.float32,
        ).astype(jnp.bfloat16)

    def finish(g, tiles, t):
        sides = [
            jnp.concatenate(
                [tiles[j][16 * u:16 * u + 16, 128 * q:128 * q + 128]
                 for j in range(8) for q in range(2)],
                axis=0,
            )
            for u in (t, t + 1)
        ]
        mixed = jnp.dot(
            spread[...], jnp.concatenate(sides, axis=1), preferred_element_type=jnp.float32
        ).astype(jnp.bfloat16)
        for h in range(2):
            out[pl.ds(16 * (t + h), 16), pl.ds(16 * g, 16), :] = (
                mixed[:, 128 * h:128 * h + 128].reshape(16, 16, LANES)
            )

    groups = picked.shape[0] // 2048
    tiles = [tile(0, j) for j in range(8)]
    for g in range(groups):
        later = []
        for t in range(0, 8, 2):
            if g + 1 < groups:
                later.append(tile(g + 1, t))
            finish(g, tiles, t)
            if g + 1 < groups:
                later.append(tile(g + 1, t + 1))
        tiles = later


def put_in_order(slot_of, arrived):
    count = slot_of.shape[0]
    width, step = 1024, 4096
    vmem = pl.BlockSpec(memory_space=pltpu.VMEM)
    picked = pl.pallas_call(
        pick_kernel,
        out_shape=jax.ShapeDtypeStruct((count, 2, LANES), jnp.bfloat16),
        in_specs=[pl.BlockSpec(memory_space=pl.ANY), vmem],
        out_specs=vmem,
        scratch_shapes=[pltpu.SMEM((width,), jnp.int32)] * 2 + [pltpu.SemaphoreType.DMA((2,))],
        compiler_params=pltpu.CompilerParams(vmem_limit_bytes=40 * 2**20),
    )(slot_of, arrived.reshape(count, 2, LANES))
    tiles = count // LANES
    turned = pl.pallas_call(
        turn_kernel,
        out_shape=jax.ShapeDtypeStruct((2 * BLOCK, 2 * tiles, LANES), jnp.bfloat16),
        grid=(count // step,),
        in_specs=[pl.BlockSpec((2 * step, LANES), lambda i: (i, 0))],
        out_specs=pl.BlockSpec((2 * BLOCK, step // BLOCK, LANES), lambda i: (0, i, 0)),
        scratch_shapes=[pltpu.VMEM((256, 256), jnp.bfloat16)] * 2,
        compiler_params=pltpu.CompilerParams(vmem_limit_bytes=40 * 2**20),
    )(picked.reshape(2 * count, LANES))
    turned = turned.reshape(2 * BLOCK, tiles, 2, LANES).transpose(0, 2, 1, 3)
    return turned.reshape(2, BLOCK, 2, count)


def per_device(strain, injections, offsets, slot_of, basis_filters, recon_matrix):
    arrived = filter_and_exchange(strain, injections, offsets, basis_filters, recon_matrix)
    return put_in_order(slot_of, arrived)


def solution(mesh):
    return jax.shard_map(
        per_device,
        mesh=mesh,
        in_specs=(
            P(None, "tm"), P(), P(), P(),
            P("bank", "cuts", None, None), P("bank", "cuts", None, None),
        ),
        out_specs=P(None, ("tm", "bank", "cuts"), None, None),
        check_vma=False,
    )
```
